32 devices in a mesh: theta: 8 (over z, core), band: 4 (over y, x).
Axes of the slice: x: 2, y: 2, z: 4, core: 2. Of those that a mesh axis runs over, the one named last changes fastest.
Arguments:
- basis: float32 [4, 5, 4, 1024], P(None, None, 'band', 'theta'), may hold values from -8 to 8
- jac_block: float32 [5, 5, 4, 1024], P(None, None, 'band', 'theta'), may hold values from -3 to 3
- face_coef: float32 [4, 5, 4, 1024], P(None, None, 'band', 'theta'), may hold values from 0.1 to 1.1
- panel_inverse: bfloat16 [4, 16, 320, 640], P('band', 'theta'), may hold values from -0.2 to 1.2
- rotor_offset: int32 [1], replicated, may hold values from 448 to 575
Outputs:
- precond: float32 [5, 4, 1024], P(None, 'band', 'theta')
- v_next: float32 [5, 4, 1024], P(None, 'band', 'theta')
- hess: float32 [5], replicated
The draws below stay inside these ranges and needn't reach their ends.
All inputs are finite; a program needn't handle non-finite values.
Results may differ from the reference program's by a relative error of at most 0.0029.
Values may be sent and summed in bfloat16 or wider, within the bound.
No kernel may reach another device: no remote copies, remote signals or barrier semaphores. Data moves between devices by JAX's collectives and lax.ppermute only.
A program may use at most 64 MiB of HBM per device.

```python
import jax
import jax.numpy as jnp
from jax import lax

NCOMP = 5
PANEL = 128
KB = 4
HALF = 64
NB = 4
NT = 1024
NPAN = 16
PROWS = 320
PCOLS = 640
IFACE = 2
NU = 20480
N_THETA = 8


def draw_basis(key, part):
    first, second = jax.random.split(jax.random.fold_in(key, 11))
    own = jax.random.normal(first, (KB, NCOMP, NB, NT), jnp.float32)
    shared = jax.random.normal(second, (1, NCOMP, NB, NT), jnp.float32)
    return jnp.clip(0.6 * own + 0.8 * shared, -8.0, 8.0)


def draw_panel_inverse(key, part):
    noise = jax.random.normal(jax.random.fold_in(key, 23), (NB, NPAN, PROWS, PCOLS), jnp.float32)
    noise = jnp.clip(noise * (0.6 / PCOLS ** 0.5), -0.19, 0.19)
    rows = jnp.arange(PROWS, dtype=jnp.int32)
    side = jnp.arange(NPAN, dtype=jnp.int32) % 2
    column = (rows // HALF)[None, :] * PANEL + (rows % HALF)[None, :] + HALF * (1 - side)[:, None]
    target = (jnp.arange(PCOLS, dtype=jnp.int32)[None, None, :] == column[:, :, None]).astype(jnp.float32)
    return (noise + target[None]).astype(jnp.bfloat16)


def block_levels(rng, shape, pieces, smallest, high):
    level, own = 1.0, jax.random.fold_in(rng, 6)
    for axis_at, parts in pieces:
        steps = jnp.exp(jax.random.uniform(jax.random.fold_in(own, axis_at), (parts,), jnp.float32, smallest / len(pieces), high / len(pieces)))
        level = level * jnp.repeat(steps, shape[axis_at] // parts).reshape([-1 if axis == axis_at else 1 for axis in range(len(shape))])
    return level


def centred(key, shape, deviation, most, pieces=(), kind=jnp.bfloat16):
    drawn = jax.random.normal(key, shape, jnp.float32) * deviation
    if len(pieces) > 0:
        drawn = block_levels(key, shape, pieces, -0.22, 0.18) * drawn
    return jnp.clip(drawn, min=-most, max=most).astype(kind)


def setup_inputs(seed: int = 0) -> dict:
    splits = jax.random.split(jax.random.key(seed), 6)
    basis = draw_basis(jax.random.fold_in(splits[5], 71), 0)
    jac_block = centred(splits[1], (NCOMP, NCOMP, NB, NT), 0.5, 3.0, ((2, 4), (3, 8)), jnp.float32)
    face_coef = jnp.clip(0.1 + 1 * jax.random.uniform(splits[2], (4, NCOMP, NB, NT), jnp.float32) ** block_levels(splits[2], (4, NCOMP, NB, NT), ((2, 4), (3, 8)), -0.2, 0.2), 0.1, 1.1)
    panel_inverse = draw_panel_inverse(jax.random.fold_in(splits[5], 71), 0)
    rotor_offset = jax.random.randint(splits[4], (1,), NT // 2 - HALF, NT // 2 + HALF).astype(jnp.int32)
    return dict(basis=basis, jac_block=jac_block, face_coef=face_coef, panel_inverse=panel_inverse, rotor_offset=rotor_offset)


def reference(basis, jac_block, face_coef, panel_inverse, rotor_offset):
    current = basis[KB - 1]
    resid16 = current.astype(jnp.bfloat16)
    starts = jnp.arange(N_THETA, dtype=jnp.int32)[:, None] * PANEL - HALF
    window = (starts + jnp.arange(2 * PANEL, dtype=jnp.int32)[None, :]) % NT
    extended = resid16[:, :, window]
    panels = extended.reshape(NCOMP, NB, N_THETA, 2, PANEL).transpose(1, 2, 3, 0, 4).reshape(NB, NPAN, PCOLS)

    def one_row(pair):
        inverse_row, panel_row = pair
        return jnp.einsum('pij,pj->pi', inverse_row.astype(jnp.float32), panel_row.astype(jnp.float32))
    owned = lax.map(one_row, (panel_inverse, panels))
    precond = owned.reshape(NB, N_THETA, 2, NCOMP, HALF).transpose(3, 0, 1, 2, 4).reshape(NCOMP, NB, NT)
    offset = rotor_offset[0]
    cells = jnp.arange(NT, dtype=jnp.int32)
    theta_minus = jnp.roll(precond, 1, axis=2)
    theta_plus = jnp.roll(precond, -1, axis=2)
    zero_row = jnp.zeros((NCOMP, 1, NT), jnp.float32)
    band_minus = jnp.concatenate([zero_row, precond[:, :-1]], axis=1)
    band_plus = jnp.concatenate([precond[:, 1:], zero_row], axis=1)
    low_shift = precond[:, IFACE - 1][:, (cells - offset + NT) % NT]
    up_shift = precond[:, IFACE][:, (cells + offset) % NT]
    band_minus = band_minus.at[:, IFACE].set(low_shift)
    band_plus = band_plus.at[:, IFACE - 1].set(up_shift)
    image = 6.0 * precond + lax.optimization_barrier(jnp.sum(jac_block * precond[None], axis=1))
    image = image - (face_coef[0] * theta_minus + face_coef[1] * theta_plus + face_coef[2] * band_minus + face_coef[3] * band_plus)
    proj = lax.optimization_barrier(jnp.sum(basis * image[None], axis=(1, 2, 3))) / NU
    ortho = image - lax.optimization_barrier(jnp.sum(proj[:, None, None, None] * basis, axis=0))
    hnorm = jnp.sqrt(jnp.sum(ortho * ortho) / NU + 1e-06)
    v_next = ortho / hnorm
    hess = jnp.concatenate([proj, hnorm[None]])
    return (precond, v_next, hess)
```

```python
import jax
import jax.numpy as jnp
from jax import lax
from jax.experimental import pallas as pl
from jax.experimental.pallas import tpu as pltpu
from jax.sharding import PartitionSpec as P

AXES = ("theta", "band")


def lane_reduced(rows):
    count, width = rows.shape
    sums = jnp.sum(rows, axis=1, keepdims=True)
    row = lax.broadcasted_iota(jnp.int32, (count, width), 0)
    lane = lax.broadcasted_iota(jnp.int32, (count, width), 1)
    return jnp.sum(jnp.where(row == lane, sums, 0.0), axis=0, keepdims=True)


def image_kernel(theta_count, band_count, offset_ref, all_ref, basis_ref, jac_ref, face_ref, image_ref, send_ref):
    kb, ncomp, _, width = basis_ref.shape
    cycle = theta_count * width
    middle = band_count // 2
    theta = lax.axis_index("theta")
    band = lax.axis_index("band")
    offset = offset_ref[0]

    def cells_of(t, b):
        t = jnp.where(t >= theta_count, t - theta_count, t)
        return all_ref[t * band_count + b].reshape(ncomp, width)

    lane = lax.broadcasted_iota(jnp.int32, (ncomp, width), 1)

    def shifted(row, shift):
        start = theta * width + shift
        first = lax.rem(start // width, theta_count)
        skip = lax.rem(start, width)
        back = lax.rem(width - skip, width)
        one = pltpu.roll(cells_of(first, row), back, 1)
        two = pltpu.roll(cells_of(first + 1, row), back, 1)
        return jnp.where(lane < width - skip, one, two)

    precond = cells_of(theta, band)
    before = cells_of(theta + theta_count - 1, band)
    after = cells_of(theta + 1, band)
    theta_minus = jnp.where(lane == 0, pltpu.roll(before, 1, 1), pltpu.roll(precond, 1, 1))
    theta_plus = jnp.where(lane == width - 1, pltpu.roll(after, width - 1, 1), pltpu.roll(precond, width - 1, 1))
    up_shift = jnp.where(band == middle - 1, offset, 0)
    low_shift = jnp.where(band == middle, cycle - offset, 0)
    band_plus = shifted(jnp.minimum(band + 1, band_count - 1), up_shift)
    band_plus = jnp.where(band == band_count - 1, 0.0, band_plus)
    band_minus = shifted(jnp.maximum(band - 1, 0), low_shift)
    band_minus = jnp.where(band == 0, 0.0, band_minus)

    coupled = jac_ref[:, 0, 0, :] * precond[0:1]
    for w in range(1, ncomp):
        coupled += jac_ref[:, w, 0, :] * precond[w : w + 1]
    image = 6.0 * precond + coupled
    image = image - (
        face_ref[0, :, 0, :] * theta_minus
        + face_ref[1, :, 0, :] * theta_plus
        + face_ref[2, :, 0, :] * band_minus
        + face_ref[3, :, 0, :] * band_plus
    )
    image_ref[...] = image
    vectors = [basis_ref[i, :, 0, :] for i in range(kb)]
    pairs = [vectors[i] * image for i in range(kb)] + [image * image]
    pairs += [vectors[i] * vectors[j] for i in range(kb) for j in range(kb)]
    rows = jnp.concatenate([jnp.sum(pair, axis=0, keepdims=True) for pair in pairs], axis=0)
    send_ref[...] = jnp.broadcast_to(lane_reduced(rows), send_ref.shape)


def finish_kernel(total, sums_ref, image_ref, basis_ref, next_ref, hess_ref):
    kb = basis_ref.shape[0]
    sums = jnp.sum(sums_ref[...], axis=0, keepdims=True) / total
    proj = [sums[0, i] for i in range(kb)]
    squares = sums[0, kb]
    for i in range(kb):
        squares -= 2.0 * proj[i] * proj[i]
    for i in range(kb):
        for j in range(kb):
            squares += proj[i] * sums[0, kb + 1 + i * kb + j] * proj[j]
    ortho = image_ref[...]
    drop = proj[0] * basis_ref[0, :, 0, :]
    for i in range(1, kb):
        drop += proj[i] * basis_ref[i, :, 0, :]
    ortho = ortho - drop
    hnorm = jnp.sqrt(jnp.full(sums.shape, squares + 1e-06, jnp.float32))
    next_ref[:, 0, :] = ortho / hnorm
    lane = lax.broadcasted_iota(jnp.int32, sums.shape, 1)
    hess_ref[...] = jnp.where(lane < kb, sums, hnorm)[:, : kb + 1]


def on_device(basis, jac_block, face_coef, panel_inverse, rotor_offset):
    kb, ncomp, rows_here, width = basis.shape
    assert rows_here == 1
    half = width // 2
    theta_count = lax.axis_size("theta")
    band_count = lax.axis_size("band")
    devices = theta_count * band_count
    total = ncomp * devices * width
    up = [(i, (i + 1) % theta_count) for i in range(theta_count)]
    down = [(j, i) for i, j in up]
    before = lax.ppermute(basis, "theta", up)[-1].astype(jnp.bfloat16)
    after = lax.ppermute(basis, "theta", down)[-1].astype(jnp.bfloat16)
    current = basis[-1].astype(jnp.bfloat16)
    extended = jnp.concatenate([before[..., half:], current, after[..., :half]], axis=2)
    panels = extended.reshape(ncomp, 2, width).transpose(1, 0, 2).reshape(2, ncomp * width)
    owned = jnp.einsum("pij,pj->pi", panel_inverse[0], panels, preferred_element_type=jnp.float32)
    precond = owned.reshape(2, ncomp, half).transpose(1, 0, 2).reshape(ncomp, 1, width)

    copies = jnp.broadcast_to(precond[None], (devices, ncomp, 1, width))
    everyone = lax.all_to_all(copies, AXES, 0, 0, tiled=True)

    smem = pl.BlockSpec(memory_space=pltpu.SMEM)
    vmem = pl.BlockSpec(memory_space=pltpu.VMEM)
    image, partial = pl.pallas_call(
        lambda *refs: image_kernel(theta_count, band_count, *refs),
        out_shape=(
            jax.ShapeDtypeStruct((ncomp, width), jnp.float32),
            jax.ShapeDtypeStruct((devices, width), jnp.float32),
        ),
        in_specs=[smem, vmem, vmem, vmem, vmem],
        out_specs=(vmem, vmem),
        name="image",
    )(rotor_offset, everyone, basis, jac_block, face_coef)
    sums = lax.all_to_all(partial, AXES, 0, 0, tiled=True)
    v_next, hess = pl.pallas_call(
        lambda *refs: finish_kernel(total, *refs),
        out_shape=(
            jax.ShapeDtypeStruct((ncomp, 1, width), jnp.float32),
            jax.ShapeDtypeStruct((1, kb + 1), jnp.float32),
        ),
        in_specs=[vmem, vmem, vmem],
        out_specs=(vmem, vmem),
        name="finish",
    )(sums, image, basis)
    return precond, v_next, hess.reshape(kb + 1)


def solution(mesh):
    return jax.shard_map(
        on_device,
        mesh=mesh,
        in_specs=(
            P(None, None, "band", "theta"),
            P(None, None, "band", "theta"),
            P(None, None, "band", "theta"),
            P("band", "theta", None, None),
            P(),
        ),
        out_specs=(P(None, "band", "theta"), P(None, "band", "theta"), P()),
        check_vma=False,
    )
```

```python
import jax
import jax.numpy as jnp
from jax import lax
from jax.experimental import pallas as pl
from jax.experimental.pallas import tpu as pltpu
from jax.sharding import PartitionSpec as P

AXES = ("theta", "band")


def lane_reduced(rows):
    count, width = rows.shape
    sums = jnp.sum(rows, axis=1, keepdims=True)
    row = lax.broadcasted_iota(jnp.int32, (count, width), 0)
    lane = lax.broadcasted_iota(jnp.int32, (count, width), 1)
    return jnp.sum(jnp.where(row == lane, sums, 0.0), axis=0, keepdims=True)


def image_kernel(theta_count, band_count, offset_ref, all_ref, basis_ref, jac_ref, face_ref, image_ref, send_ref):
    kb, ncomp, _, width = basis_ref.shape
    cycle = theta_count * width
    middle = band_count // 2
    theta = lax.axis_index("theta")
    band = lax.axis_index("band")
    offset = offset_ref[0]

    def cells_of(t, b):
        t = jnp.where(t >= theta_count, t - theta_count, t)
        return all_ref[t * band_count + b].reshape(ncomp, width)

    lane = lax.broadcasted_iota(jnp.int32, (ncomp, width), 1)

    def shifted(row, shift):
        start = theta * width + shift
        first = lax.rem(start // width, theta_count)
        skip = lax.rem(start, width)
        back = lax.rem(width - skip, width)
        one = pltpu.roll(cells_of(first, row), back, 1)
        two = pltpu.roll(cells_of(first + 1, row), back, 1)
        return jnp.where(lane < width - skip, one, two)

    precond = cells_of(theta, band)
    before = cells_of(theta + theta_count - 1, band)
    after = cells_of(theta + 1, band)
    theta_minus = jnp.where(lane == 0, pltpu.roll(before, 1, 1), pltpu.roll(precond, 1, 1))
    theta_plus = jnp.where(lane == width - 1, pltpu.roll(after, width - 1, 1), pltpu.roll(precond, width - 1, 1))
    up_shift = jnp.where(band == middle - 1, offset, 0)
    low_shift = jnp.where(band == middle, cycle - offset, 0)
    band_plus = shifted(jnp.minimum(band + 1, band_count - 1), up_shift)
    band_plus = jnp.where(band == band_count - 1, 0.0, band_plus)
    band_minus = shifted(jnp.maximum(band - 1, 0), low_shift)
    band_minus = jnp.where(band == 0, 0.0, band_minus)

    coupled = jac_ref[:, 0, 0, :] * precond[0:1]
    for w in range(1, ncomp):
        coupled += jac_ref[:, w, 0, :] * precond[w : w + 1]
    image = 6.0 * precond + coupled
    image = image - (
        face_ref[0, :, 0, :] * theta_minus
        + face_ref[1, :, 0, :] * theta_plus
        + face_ref[2, :, 0, :] * band_minus
        + face_ref[3, :, 0, :] * band_plus
    )
    image_ref[...] = image
    vectors = [basis_ref[i, :, 0, :] for i in range(kb)]
    pairs = [vectors[i] * image for i in range(kb)] + [image * image]
    pairs += [vectors[i] * vectors[j] for i in range(kb) for j in range(kb)]
    rows = jnp.concatenate([jnp.sum(pair, axis=0, keepdims=True) for pair in pairs], axis=0)
    send_ref[...] = jnp.broadcast_to(lane_reduced(rows), send_ref.shape)


def finish_kernel(total, sums_ref, image_ref, basis_ref, next_ref, hess_ref):
    kb = basis_ref.shape[0]
    sums = jnp.sum(sums_ref[...], axis=0, keepdims=True) / total
    proj = [sums[0, i] for i in range(kb)]
    squares = sums[0, kb]
    for i in range(kb):
        squares -= 2.0 * proj[i] * proj[i]
    for i in range(kb):
        for j in range(kb):
            squares += proj[i] * sums[0, kb + 1 + i * kb + j] * proj[j]
    ortho = image_ref[...]
    drop = proj[0] * basis_ref[0, :, 0, :]
    for i in range(1, kb):
        drop += proj[i] * basis_ref[i, :, 0, :]
    ortho = ortho - drop
    hnorm = jnp.sqrt(jnp.full(sums.shape, squares + 1e-06, jnp.float32))
    next_ref[:, 0, :] = ortho / hnorm
    lane = lax.broadcasted_iota(jnp.int32, sums.shape, 1)
    hess_ref[...] = jnp.where(lane < kb, sums, hnorm)[:, : kb + 1]


def on_device(basis, jac_block, face_coef, panel_inverse, rotor_offset):
    kb, ncomp, rows_here, width = basis.shape
    assert rows_here == 1
    half = width // 2
    theta_count = lax.axis_size("theta")
    band_count = lax.axis_size("band")
    devices = theta_count * band_count
    total = ncomp * devices * width
    up = [(i, (i + 1) % theta_count) for i in range(theta_count)]
    down = [(j, i) for i, j in up]
    before = lax.ppermute(basis, "theta", up)[-1].astype(jnp.bfloat16)
    after = lax.ppermute(basis, "theta", down)[-1].astype(jnp.bfloat16)
    current = basis[-1].astype(jnp.bfloat16)
    extended = jnp.concatenate([before[..., half:], current, after[..., :half]], axis=2)
    panels = extended.reshape(ncomp, 2, width).transpose(1, 0, 2).reshape(2, ncomp * width)
    owned = jnp.einsum("pij,pj->pi", panel_inverse[0], panels, preferred_element_type=jnp.float32)
    precond = owned.reshape(2, ncomp, half).transpose(1, 0, 2).reshape(ncomp, 1, width)

    copies = jnp.broadcast_to(precond[None], (devices, ncomp, 1, width))
    everyone = lax.all_to_all(copies, AXES, 0, 0, tiled=True)

    smem = pl.BlockSpec(memory_space=pltpu.SMEM)
    vmem = pl.BlockSpec(memory_space=pltpu.VMEM)
    image, partial = pl.pallas_call(
        lambda *refs: image_kernel(theta_count, band_count, *refs),
        out_shape=(
            pltpu.VMEM((ncomp, width), jnp.float32),
            pltpu.VMEM((devices, width), jnp.float32),
        ),
        in_specs=[smem, vmem, vmem, vmem, vmem],
        out_specs=(vmem, vmem),
        name="image",
    )(rotor_offset, *[pltpu.with_memory_space_constraint(v, pltpu.VMEM) for v in (everyone, basis, jac_block, face_coef)])
    sums = lax.all_to_all(partial, AXES, 0, 0, tiled=True)
    v_next, hess = pl.pallas_call(
        lambda *refs: finish_kernel(total, *refs),
        out_shape=(
            jax.ShapeDtypeStruct((ncomp, 1, width), jnp.float32),
            jax.ShapeDtypeStruct((1, kb + 1), jnp.float32),
        ),
        in_specs=[vmem, vmem, vmem],
        out_specs=(vmem, vmem),
        name="finish",
    )(*[pltpu.with_memory_space_constraint(v, pltpu.VMEM) for v in (sums, image, basis)])
    return precond, v_next, hess.reshape(kb + 1)


def solution(mesh):
    return jax.shard_map(
        on_device,
        mesh=mesh,
        in_specs=(
            P(None, None, "band", "theta"),
            P(None, None, "band", "theta"),
            P(None, None, "band", "theta"),
            P("band", "theta", None, None),
            P(),
        ),
        out_specs=(P(None, "band", "theta"), P(None, "band", "theta"), P()),
        check_vma=False,
    )
```

```python
import jax
import jax.numpy as jnp
from jax import lax
from jax.experimental import pallas as pl
from jax.experimental.pallas import tpu as pltpu
from jax.sharding import PartitionSpec as P

AXES = ("theta", "band")
MERGED_LIMIT = 64
THIRD = 32


def even(count):
    return -(-count // 2) * 2


def in_vmem(*arrays):
    return [pltpu.with_memory_space_constraint(array, pltpu.VMEM) for array in arrays]


def specs(count, scalars=0):
    smem = pl.BlockSpec(memory_space=pltpu.SMEM)
    vmem = pl.BlockSpec(memory_space=pltpu.VMEM)
    return [smem] * scalars + [vmem] * count


def lane_reduced(rows):
    count, width = rows.shape
    sums = jnp.sum(rows, axis=1, keepdims=True)
    row = lax.broadcasted_iota(jnp.int32, (count, width), 0)
    lane = lax.broadcasted_iota(jnp.int32, (count, width), 1)
    return jnp.sum(jnp.where(row == lane, sums, 0.0), axis=0, keepdims=True)


def coupled(jac_ref, precond):
    out = jac_ref[:, 0, 0, :] * precond[0:1]
    for w in range(1, precond.shape[0]):
        out += jac_ref[:, w, 0, :] * precond[w : w + 1]
    return out


def over_cells(arrays):
    return [jnp.sum(array, axis=0, keepdims=True) for array in arrays]


def finished(proj, gram, square, image, basis_ref, next_ref, hess_ref):
    kb = basis_ref.shape[0]
    squares = square
    for i in range(kb):
        squares -= 2.0 * proj[i] * proj[i]
    for i in range(kb):
        for j in range(kb):
            squares += proj[i] * gram[i * kb + j] * proj[j]
    drop = proj[0] * basis_ref[0, :, 0, :]
    for i in range(1, kb):
        drop += proj[i] * basis_ref[i, :, 0, :]
    row = (1, image.shape[1])
    hnorm = jnp.sqrt(jnp.full(row, squares + 1e-06, jnp.float32))
    next_ref[:, 0, :] = (image - drop) / hnorm
    lane = lax.broadcasted_iota(jnp.int32, row, 1)
    hess = hnorm
    for i in range(kb):
        hess = jnp.where(lane == i, proj[i], hess)
    hess_ref[...] = hess[:, : kb + 1]


def image_kernel(theta_count, band_count, offset_ref, all_ref, basis_ref, jac_ref, face_ref, image_ref, send_ref):
    kb, ncomp, _, width = basis_ref.shape
    cycle = theta_count * width
    middle = band_count // 2
    theta = lax.axis_index("theta")
    band = lax.axis_index("band")
    offset = offset_ref[0]

    def cells_of(t, b):
        t = jnp.where(t >= theta_count, t - theta_count, t)
        return all_ref[t * band_count + b].reshape(ncomp, width)

    lane = lax.broadcasted_iota(jnp.int32, (ncomp, width), 1)

    def shifted(row, shift):
        start = theta * width + shift
        first = lax.rem(start // width, theta_count)
        skip = lax.rem(start, width)
        back = lax.rem(width - skip, width)
        one = pltpu.roll(cells_of(first, row), back, 1)
        two = pltpu.roll(cells_of(first + 1, row), back, 1)
        return jnp.where(lane < width - skip, one, two)

    precond = cells_of(theta, band)
    before = cells_of(theta + theta_count - 1, band)
    after = cells_of(theta + 1, band)
    theta_minus = jnp.where(lane == 0, pltpu.roll(before, 1, 1), pltpu.roll(precond, 1, 1))
    theta_plus = jnp.where(lane == width - 1, pltpu.roll(after, width - 1, 1), pltpu.roll(precond, width - 1, 1))
    up_shift = jnp.where(band == middle - 1, offset, 0)
    low_shift = jnp.where(band == middle, cycle - offset, 0)
    band_plus = shifted(jnp.minimum(band + 1, band_count - 1), up_shift)
    band_plus = jnp.where(band == band_count - 1, 0.0, band_plus)
    band_minus = shifted(jnp.maximum(band - 1, 0), low_shift)
    band_minus = jnp.where(band == 0, 0.0, band_minus)
    image = 6.0 * precond + coupled(jac_ref, precond)
    image = image - (
        face_ref[0, :, 0, :] * theta_minus
        + face_ref[1, :, 0, :] * theta_plus
        + face_ref[2, :, 0, :] * band_minus
        + face_ref[3, :, 0, :] * band_plus
    )
    image_ref[...] = image
    vectors = [basis_ref[i, :, 0, :] for i in range(kb)]
    pairs = [vectors[i] * image for i in range(kb)] + [image * image]
    pairs += [vectors[i] * vectors[j] for i in range(kb) for j in range(kb)]
    rows = jnp.concatenate(over_cells(pairs), axis=0)
    send_ref[...] = jnp.broadcast_to(lane_reduced(rows), send_ref.shape)


def finish_kernel(total, sums_ref, image_ref, basis_ref, next_ref, hess_ref):
    kb = basis_ref.shape[0]
    sums = jnp.sum(sums_ref[...], axis=0, keepdims=True) / total
    proj = [sums[0, i] for i in range(kb)]
    gram = [sums[0, kb + 1 + i] for i in range(kb * kb)]
    finished(proj, gram, sums[0, kb], image_ref[...], basis_ref, next_ref, hess_ref)


def two_exchanges(precond, basis, jac_block, face_coef, rotor_offset):
    kb, ncomp, _, width = basis.shape
    theta_count = lax.axis_size("theta")
    band_count = lax.axis_size("band")
    devices = theta_count * band_count
    copies = jnp.broadcast_to(precond[None], (devices, ncomp, 1, width))
    everyone = lax.all_to_all(copies, AXES, 0, 0, tiled=True)
    image, partial = pl.pallas_call(
        lambda *refs: image_kernel(theta_count, band_count, *refs),
        out_shape=(pltpu.VMEM((ncomp, width), jnp.float32), pltpu.VMEM((devices, width), jnp.float32)),
        in_specs=specs(4, 1),
        out_specs=specs(2),
        name="image",
    )(rotor_offset, *in_vmem(everyone, basis, jac_block, face_coef))
    sums = lax.all_to_all(partial, AXES, 0, 0, tiled=True)
    total = ncomp * devices * width
    return pl.pallas_call(
        lambda *refs: finish_kernel(total, *refs),
        out_shape=(
            jax.ShapeDtypeStruct((ncomp, 1, width), jnp.float32),
            jax.ShapeDtypeStruct((1, kb + 1), jnp.float32),
        ),
        in_specs=specs(3),
        out_specs=specs(2),
        name="finish",
    )(*in_vmem(sums, image, basis))


def thirds(x):
    high = x.astype(jnp.bfloat16).astype(jnp.float32)
    middle = (x - high).astype(jnp.bfloat16).astype(jnp.float32)
    return high, middle, x - high - middle


def message_rows(kb, ncomp):
    return even((4 + kb) * ncomp + 1)


def local_kernel(precond_ref, basis_ref, jac_ref, face_ref, send_ref, inner_ref, out_ref):
    kb, ncomp, _, width = basis_ref.shape
    slot = message_rows(kb, ncomp)
    precond = precond_ref[...]
    out_ref[:, 0, :] = precond
    lane = lax.broadcasted_iota(jnp.int32, (ncomp, width), 1)
    lower = jnp.where(lane == 0, 0.0, pltpu.roll(precond, 1, 1))
    upper = jnp.where(lane == width - 1, 0.0, pltpu.roll(precond, width - 1, 1))
    inner = 6.0 * precond + coupled(jac_ref, precond)
    inner = inner - (face_ref[0, :, 0, :] * lower + face_ref[1, :, 0, :] * upper)
    inner_ref[...] = inner
    vectors = [basis_ref[i, :, 0, :] for i in range(kb)]
    pairs = [vectors[i] * inner for i in range(kb)] + [inner * inner]
    pairs += [vectors[i] * vectors[j] for i in range(kb) for j in range(kb)]
    rows = jnp.concatenate(over_cells(pairs), axis=0)
    high, middle, low = thirds(lane_reduced(rows))
    sums = high + pltpu.roll(middle, THIRD, 1) + pltpu.roll(low, 2 * THIRD, 1)
    row = lax.broadcasted_iota(jnp.int32, (ncomp, width), 0)
    first = jnp.where(lane == 3 * THIRD + row, face_ref[0, :, 0, :][:, :1], 0.0)
    last = jnp.where(lane == 3 * THIRD + THIRD // 2 + row, face_ref[1, :, 0, :][:, width - 1 :], 0.0)
    sums += jnp.sum(first + last, axis=0, keepdims=True)
    groups = [face_ref[2, :, 0, :], face_ref[3, :, 0, :], *vectors, inner, precond, sums]
    if slot > (4 + kb) * ncomp + 1:
        groups.append(jnp.zeros((slot - (4 + kb) * ncomp - 1, width), jnp.float32))
    message = jnp.concatenate(groups, axis=0).astype(jnp.bfloat16)
    for device in range(send_ref.shape[0] // slot):
        send_ref[device * slot : (device + 1) * slot] = message


def merged_kernel(theta_count, band_count, offset_ref, all_ref, inner_ref, basis_ref, face_ref, next_ref, hess_ref, own_ref):
    kb, ncomp, _, width = basis_ref.shape
    devices = theta_count * band_count
    cycle = theta_count * width
    total = ncomp * devices * width
    middle = band_count // 2
    shape = (devices, width)
    row = lax.broadcasted_iota(jnp.int32, shape, 0)
    lane = lax.broadcasted_iota(jnp.int32, shape, 1)
    band = lax.rem(row, band_count)
    here = lax.axis_index("theta") * band_count + lax.axis_index("band")
    base = cycle // 2 - width
    start = offset_ref[0] - base
    late = start >= width
    skip = jnp.where(late, start - width, start)

    def part(place):
        return all_ref[pl.ds(place, devices, stride=all_ref.shape[0] // devices), :]

    def rows_up(x, count):
        return pltpu.roll(x, (devices - count) % devices, 0)

    half = theta_count // 2
    local = part((4 + kb) * ncomp)
    square = jnp.zeros(shape, jnp.float32)
    cross = [jnp.zeros(shape, jnp.float32) for _ in range(kb)]
    for u in range(ncomp):
        inner, precond = part((2 + kb) * ncomp + u), part((3 + kb) * ncomp + u)
        turned = pltpu.roll(precond, lax.rem(width - skip, width), 1)
        near, at, far = (rows_up(turned, (half + k) * band_count + 1) for k in (-1, 0, 1))
        split = lane < width - skip
        rotor_up = jnp.where(split, jnp.where(late, at, near), jnp.where(late, far, at))
        turned = pltpu.roll(precond, skip, 1)
        near, at, far = (rows_up(turned, (-half + k) * band_count - 1) for k in (1, 0, -1))
        split = lane >= skip
        rotor_down = jnp.where(split, jnp.where(late, at, near), jnp.where(late, far, at))
        band_plus = jnp.where(band == middle - 1, rotor_up, rows_up(precond, 1))
        band_plus = jnp.where(band == band_count - 1, 0.0, band_plus)
        band_minus = jnp.where(band == middle, rotor_down, rows_up(precond, -1))
        band_minus = jnp.where(band == 0, 0.0, band_minus)
        before = rows_up(pltpu.roll(precond, 1, 1), -band_count)
        after = rows_up(pltpu.roll(precond, width - 1, 1), band_count)
        edge = jnp.where(lane == 0, before, after)
        place = 3 * THIRD + u
        first = pltpu.roll(local, width - place, 1)
        last = pltpu.roll(local, width - 1 - place - THIRD // 2, 1)
        coef = jnp.where(lane == 0, first, jnp.where(lane == width - 1, last, 0.0))
        own_ref[0, u] = band_minus
        own_ref[1, u] = band_plus
        own_ref[2, u] = edge
        outer = part(u) * band_minus + part(ncomp + u) * band_plus + coef * edge
        square += outer * (outer - 2.0 * inner)
        for i in range(kb):
            cross[i] += part((2 + i) * ncomp + u) * outer
    local = jnp.sum(local, axis=0, keepdims=True) / total
    local = local + pltpu.roll(local, width - THIRD, 1) + pltpu.roll(local, width - 2 * THIRD, 1)
    sums = lane_reduced(jnp.concatenate(over_cells(cross + [square]), axis=0)) / total
    proj = [local[0, i] - sums[0, i] for i in range(kb)]
    gram = [local[0, kb + 1 + i] for i in range(kb * kb)]

    def own(k):
        return own_ref[k, :, pl.ds(here, 1), :].reshape(ncomp, width)

    lane = lax.broadcasted_iota(jnp.int32, (ncomp, width), 1)
    edges = jnp.where(lane == 0, face_ref[0, :, 0, :], jnp.where(lane == width - 1, face_ref[1, :, 0, :], 0.0))
    outer = face_ref[2, :, 0, :] * own(0) + face_ref[3, :, 0, :] * own(1) + edges * own(2)
    finished(proj, gram, local[0, kb] + sums[0, kb], inner_ref[...] - outer, basis_ref, next_ref, hess_ref)


def one_exchange(precond, basis, jac_block, face_coef, rotor_offset):
    kb, ncomp, _, width = basis.shape
    theta_count = lax.axis_size("theta")
    band_count = lax.axis_size("band")
    devices = theta_count * band_count
    send, inner, precond = pl.pallas_call(
        local_kernel,
        out_shape=(
            jax.ShapeDtypeStruct((devices * message_rows(kb, ncomp), width), jnp.bfloat16),
            pltpu.VMEM((ncomp, width), jnp.float32),
            jax.ShapeDtypeStruct((ncomp, 1, width), jnp.float32),
        ),
        in_specs=specs(4),
        out_specs=specs(3),
        name="local",
    )(*in_vmem(precond.reshape(ncomp, width), basis, jac_block, face_coef))
    everyone = exchanged(send, devices)
    everyone = everyone.astype(jnp.float32)
    v_next, hess = pl.pallas_call(
        lambda *refs: merged_kernel(theta_count, band_count, *refs),
        out_shape=(
            jax.ShapeDtypeStruct((ncomp, 1, width), jnp.float32),
            jax.ShapeDtypeStruct((1, kb + 1), jnp.float32),
        ),
        in_specs=specs(4, 1),
        out_specs=specs(2),
        scratch_shapes=[pltpu.VMEM((3, ncomp, devices, width), jnp.float32)],
        name="merged",
    )(rotor_offset, *in_vmem(everyone, inner, basis, face_coef))
    return precond, v_next, hess


def exchanged(rows, devices):
    slots = rows.reshape(devices, -1, 2, rows.shape[-1])
    return lax.all_to_all(slots, AXES, 0, 0, tiled=True).reshape(rows.shape)


def on_device(basis, jac_block, face_coef, panel_inverse, rotor_offset):
    kb, ncomp, rows_here, width = basis.shape
    assert rows_here == 1
    half = width // 2
    theta_count = lax.axis_size("theta")
    band_count = lax.axis_size("band")
    merged = theta_count * band_count <= MERGED_LIMIT
    up = [(i, (i + 1) % theta_count) for i in range(theta_count)]
    down = [(j, i) for i, j in up]
    before = lax.ppermute(basis, "theta", up)
    after = lax.ppermute(basis, "theta", down)
    before, current, after = (x[-1].astype(jnp.bfloat16) for x in (before, basis, after))
    extended = jnp.concatenate([before[..., half:], current, after[..., :half]], axis=2)
    panels = extended.reshape(ncomp, 2, width).transpose(1, 0, 2).reshape(2, ncomp * width)
    owned = jnp.einsum("pij,pj->pi", panel_inverse[0], panels, preferred_element_type=jnp.float32)
    precond = owned.reshape(2, ncomp, half).transpose(1, 0, 2).reshape(ncomp, 1, width)
    if merged:
        precond, v_next, hess = one_exchange(precond, basis, jac_block, face_coef, rotor_offset)
    else:
        v_next, hess = two_exchanges(precond, basis, jac_block, face_coef, rotor_offset)
    return precond, v_next, hess.reshape(kb + 1)


def solution(mesh):
    return jax.shard_map(
        on_device,
        mesh=mesh,
        in_specs=(
            P(None, None, "band", "theta"),
            P(None, None, "band", "theta"),
            P(None, None, "band", "theta"),
            P("band", "theta", None, None),
            P(),
        ),
        out_specs=(P(None, "band", "theta"), P(None, "band", "theta"), P()),
        check_vma=False,
    )
```

```python
import jax
import jax.numpy as jnp
from jax import lax
from jax.experimental import pallas as pl
from jax.experimental.pallas import tpu as pltpu
from jax.sharding import PartitionSpec as P


AXES = ("theta", "band")
MERGED_LIMIT = 64
THIRD = 32


def even(count):
    return -(-count // 2) * 2


def in_vmem(*arrays):
    return [pltpu.with_memory_space_constraint(array, pltpu.VMEM) for array in arrays]


def specs(count, scalars=0):
    smem = pl.BlockSpec(memory_space=pltpu.SMEM)
    vmem = pl.BlockSpec(memory_space=pltpu.VMEM)
    return [smem] * scalars + [vmem] * count


def lane_reduced(rows):
    count, width = rows.shape
    sums = jnp.sum(rows, axis=1, keepdims=True)
    row = lax.broadcasted_iota(jnp.int32, (count, width), 0)
    lane = lax.broadcasted_iota(jnp.int32, (count, width), 1)
    return jnp.sum(jnp.where(row == lane, sums, 0.0), axis=0, keepdims=True)


def coupled(jac_ref, precond):
    out = jac_ref[:, 0, 0, :] * precond[0:1]
    for w in range(1, precond.shape[0]):
        out += jac_ref[:, w, 0, :] * precond[w : w + 1]
    return out


def over_cells(arrays):
    return [jnp.sum(array, axis=0, keepdims=True) for array in arrays]


def finished(proj, gram, square, image, basis_ref, next_ref, hess_ref):
    kb = basis_ref.shape[0]
    squares = square
    for i in range(kb):
        squares -= 2.0 * proj[i] * proj[i]
    for i in range(kb):
        for j in range(kb):
            squares += proj[i] * gram[i * kb + j] * proj[j]
    drop = proj[0] * basis_ref[0, :, 0, :]
    for i in range(1, kb):
        drop += proj[i] * basis_ref[i, :, 0, :]
    row = (1, image.shape[1])
    hnorm = jnp.sqrt(jnp.full(row, squares + 1e-06, jnp.float32))
    next_ref[:, 0, :] = (image - drop) / hnorm
    lane = lax.broadcasted_iota(jnp.int32, row, 1)
    hess = hnorm
    for i in range(kb):
        hess = jnp.where(lane == i, proj[i], hess)
    hess_ref[...] = hess[:, : kb + 1]


def image_kernel(theta_count, band_count, offset_ref, all_ref, basis_ref, jac_ref, face_ref, image_ref, send_ref):
    kb, ncomp, _, width = basis_ref.shape
    cycle = theta_count * width
    middle = band_count // 2
    theta = lax.axis_index("theta")
    band = lax.axis_index("band")
    offset = offset_ref[0]

    def cells_of(t, b):
        t = jnp.where(t >= theta_count, t - theta_count, t)
        return all_ref[t * band_count + b].reshape(ncomp, width)

    lane = lax.broadcasted_iota(jnp.int32, (ncomp, width), 1)

    def shifted(row, shift):
        start = theta * width + shift
        first = lax.rem(start // width, theta_count)
        skip = lax.rem(start, width)
        back = lax.rem(width - skip, width)
        one = pltpu.roll(cells_of(first, row), back, 1)
        two = pltpu.roll(cells_of(first + 1, row), back, 1)
        return jnp.where(lane < width - skip, one, two)

    precond = cells_of(theta, band)
    before = cells_of(theta + theta_count - 1, band)
    after = cells_of(theta + 1, band)
    theta_minus = jnp.where(lane == 0, pltpu.roll(before, 1, 1), pltpu.roll(precond, 1, 1))
    theta_plus = jnp.where(lane == width - 1, pltpu.roll(after, width - 1, 1), pltpu.roll(precond, width - 1, 1))
    up_shift = jnp.where(band == middle - 1, offset, 0)
    low_shift = jnp.where(band == middle, cycle - offset, 0)
    band_plus = shifted(jnp.minimum(band + 1, band_count - 1), up_shift)
    band_plus = jnp.where(band == band_count - 1, 0.0, band_plus)
    band_minus = shifted(jnp.maximum(band - 1, 0), low_shift)
    band_minus = jnp.where(band == 0, 0.0, band_minus)
    image = 6.0 * precond + coupled(jac_ref, precond)
    image = image - (
        face_ref[0, :, 0, :] * theta_minus
        + face_ref[1, :, 0, :] * theta_plus
        + face_ref[2, :, 0, :] * band_minus
        + face_ref[3, :, 0, :] * band_plus
    )
    image_ref[...] = image
    vectors = [basis_ref[i, :, 0, :] for i in range(kb)]
    pairs = [vectors[i] * image for i in range(kb)] + [image * image]
    pairs += [vectors[i] * vectors[j] for i in range(kb) for j in range(kb)]
    rows = jnp.concatenate(over_cells(pairs), axis=0)
    send_ref[...] = jnp.broadcast_to(lane_reduced(rows), send_ref.shape)


def finish_kernel(total, sums_ref, image_ref, basis_ref, next_ref, hess_ref):
    kb = basis_ref.shape[0]
    sums = jnp.sum(sums_ref[...], axis=0, keepdims=True) / total
    proj = [sums[0, i] for i in range(kb)]
    gram = [sums[0, kb + 1 + i] for i in range(kb * kb)]
    finished(proj, gram, sums[0, kb], image_ref[...], basis_ref, next_ref, hess_ref)


def two_exchanges(precond, basis, jac_block, face_coef, rotor_offset):
    kb, ncomp, _, width = basis.shape
    theta_count = lax.axis_size("theta")
    band_count = lax.axis_size("band")
    devices = theta_count * band_count
    copies = jnp.broadcast_to(precond[None], (devices, ncomp, 1, width))
    everyone = lax.all_to_all(copies, AXES, 0, 0, tiled=True)
    image, partial = pl.pallas_call(
        lambda *refs: image_kernel(theta_count, band_count, *refs),
        out_shape=(pltpu.VMEM((ncomp, width), jnp.float32), pltpu.VMEM((devices, width), jnp.float32)),
        in_specs=specs(4, 1),
        out_specs=specs(2),
        name="image",
    )(rotor_offset, *in_vmem(everyone, basis, jac_block, face_coef))
    sums = lax.all_to_all(partial, AXES, 0, 0, tiled=True)
    total = ncomp * devices * width
    return pl.pallas_call(
        lambda *refs: finish_kernel(total, *refs),
        out_shape=(
            jax.ShapeDtypeStruct((ncomp, 1, width), jnp.float32),
            jax.ShapeDtypeStruct((1, kb + 1), jnp.float32),
        ),
        in_specs=specs(3),
        out_specs=specs(2),
        name="finish",
    )(*in_vmem(sums, image, basis))


def thirds(x):
    high = x.astype(jnp.bfloat16).astype(jnp.float32)
    middle = (x - high).astype(jnp.bfloat16).astype(jnp.float32)
    return high, middle, x - high - middle


def message_rows(kb, ncomp):
    return even((4 + kb) * ncomp + 1)


def early_kernel(
    basis_hbm, jac_hbm, face_hbm, panel_hbm, static_ref, sums_ref, block_ref, basis_ref, face_ref, panel_ref, jac_ref, sems
):
    pairs = ((basis_hbm, basis_ref), (jac_hbm, jac_ref), (face_hbm, face_ref), (panel_hbm, panel_ref))
    copies = [pltpu.make_async_copy(source, target, sems.at[i]) for i, (source, target) in enumerate(pairs)]
    for copy in copies:
        copy.start()
    for copy in copies[:3]:
        copy.wait()
    kb, ncomp, _, width = basis_ref.shape
    vectors = [basis_ref[i, :, 0, :] for i in range(kb)]
    pairs = [vectors[i] * vectors[j] for i in range(kb) for j in range(kb)]
    blank = [jnp.zeros((1, width), jnp.float32)] * (kb + 1)
    rows = jnp.concatenate(blank + over_cells(pairs), axis=0)
    high, middle, low = thirds(lane_reduced(rows))
    sums = high + pltpu.roll(middle, THIRD, 1) + pltpu.roll(low, 2 * THIRD, 1)
    row = lax.broadcasted_iota(jnp.int32, (ncomp, width), 0)
    lane = lax.broadcasted_iota(jnp.int32, (ncomp, width), 1)
    first = jnp.where(lane == 3 * THIRD + row, face_ref[0, :, 0, :][:, :1], 0.0)
    last = jnp.where(lane == 3 * THIRD + THIRD // 2 + row, face_ref[1, :, 0, :][:, width - 1 :], 0.0)
    sums_ref[...] = sums + jnp.sum(first + last, axis=0, keepdims=True)
    static_ref[...] = jnp.concatenate([face_ref[2, :, 0, :], face_ref[3, :, 0, :], *vectors], axis=0)
    for w in range(ncomp):
        block_ref[w] = jac_ref[:, w, 0, :] + jnp.where(row == w, 6.0, 0.0)
    copies[3].wait()


def local_kernel(
    before_ref, after_ref, panel_ref, basis_ref, face_ref, static_ref, sums_ref, block_ref, send_ref, inner_ref, out_ref
):
    kb, ncomp, _, width = basis_ref.shape
    half = width // 2
    slot = message_rows(kb, ncomp)
    lane = lax.broadcasted_iota(jnp.int32, (ncomp, width), 1)
    current = basis_ref[kb - 1, :, 0, :]
    swapped = pltpu.roll(current, half, 1)
    left = jnp.where(lane < half, pltpu.roll(before_ref[kb - 1, :, 0, :], half, 1), swapped)
    right = jnp.where(lane < half, swapped, pltpu.roll(after_ref[kb - 1, :, 0, :], half, 1))
    owned = []
    for h, cells in enumerate((left, right)):
        vector = jnp.concatenate([jnp.broadcast_to(cells[u : u + 1], (8, width)) for u in range(ncomp)], axis=1)
        owned.append(
            lax.dot_general(
                vector.astype(jnp.bfloat16),
                panel_ref[0, h],
                (((1,), (1,)), ((), ())),
                preferred_element_type=jnp.float32,
            )[:1]
        )
    halves = [[owned[h][:, u * half : (u + 1) * half] for u in range(ncomp)] for h in range(2)]
    precond = jnp.concatenate([jnp.concatenate([halves[0][u], halves[1][u]], axis=1) for u in range(ncomp)], axis=0)
    out_ref[:, 0, :] = precond
    lower = jnp.where(lane == 0, 0.0, pltpu.roll(precond, 1, 1))
    upper = jnp.where(lane == width - 1, 0.0, pltpu.roll(precond, width - 1, 1))
    inner = block_ref[0] * precond[0:1]
    for w in range(1, ncomp):
        inner += block_ref[w] * precond[w : w + 1]
    inner = inner - (face_ref[0, :, 0, :] * lower + face_ref[1, :, 0, :] * upper)
    inner_ref[...] = inner
    pairs = [basis_ref[i, :, 0, :] * inner for i in range(kb)] + [inner * inner]
    high, middle, low = thirds(lane_reduced(jnp.concatenate(over_cells(pairs), axis=0)))
    sums = sums_ref[...] + high + pltpu.roll(middle, THIRD, 1) + pltpu.roll(low, 2 * THIRD, 1)
    groups = [static_ref[...], inner, precond, sums]
    if slot > (4 + kb) * ncomp + 1:
        groups.append(jnp.zeros((slot - (4 + kb) * ncomp - 1, width), jnp.float32))
    message = jnp.concatenate(groups, axis=0).astype(jnp.bfloat16)
    for device in range(send_ref.shape[0] // slot):
        send_ref[device * slot : (device + 1) * slot] = message


def merged_kernel(theta_count, band_count, offset_ref, all_ref, inner_ref, basis_ref, face_ref, next_ref, hess_ref, own_ref):
    kb, ncomp, _, width = basis_ref.shape
    devices = theta_count * band_count
    cycle = theta_count * width
    total = ncomp * devices * width
    middle = band_count // 2
    shape = (devices, width)
    row = lax.broadcasted_iota(jnp.int32, shape, 0)
    lane = lax.broadcasted_iota(jnp.int32, shape, 1)
    band = lax.rem(row, band_count)
    here = lax.axis_index("theta") * band_count + lax.axis_index("band")
    base = cycle // 2 - width
    start = offset_ref[0] - base
    late = start >= width
    skip = jnp.where(late, start - width, start)

    def part(place):
        return all_ref[pl.ds(place, devices, stride=all_ref.shape[0] // devices), :]

    def rows_up(x, count):
        return pltpu.roll(x, (devices - count) % devices, 0)

    half = theta_count // 2
    local = part((4 + kb) * ncomp)
    square = jnp.zeros(shape, jnp.float32)
    cross = [jnp.zeros(shape, jnp.float32) for _ in range(kb)]
    for u in range(ncomp):
        inner, precond = part((2 + kb) * ncomp + u), part((3 + kb) * ncomp + u)
        turned = pltpu.roll(precond, lax.rem(width - skip, width), 1)
        near, at, far = (rows_up(turned, (half + k) * band_count + 1) for k in (-1, 0, 1))
        split = lane < width - skip
        rotor_up = jnp.where(split, jnp.where(late, at, near), jnp.where(late, far, at))
        turned = pltpu.roll(precond, skip, 1)
        near, at, far = (rows_up(turned, (-half + k) * band_count - 1) for k in (1, 0, -1))
        split = lane >= skip
        rotor_down = jnp.where(split, jnp.where(late, at, near), jnp.where(late, far, at))
        band_plus = jnp.where(band == middle - 1, rotor_up, rows_up(precond, 1))
        band_plus = jnp.where(band == band_count - 1, 0.0, band_plus)
        band_minus = jnp.where(band == middle, rotor_down, rows_up(precond, -1))
        band_minus = jnp.where(band == 0, 0.0, band_minus)
        before = rows_up(pltpu.roll(precond, 1, 1), -band_count)
        after = rows_up(pltpu.roll(precond, width - 1, 1), band_count)
        edge = jnp.where(lane == 0, before, after)
        place = 3 * THIRD + u
        first = pltpu.roll(local, width - place, 1)
        last = pltpu.roll(local, width - 1 - place - THIRD // 2, 1)
        coef = jnp.where(lane == 0, first, jnp.where(lane == width - 1, last, 0.0))
        own_ref[0, u] = band_minus
        own_ref[1, u] = band_plus
        own_ref[2, u] = edge
        outer = part(u) * band_minus + part(ncomp + u) * band_plus + coef * edge
        square += outer * (outer - 2.0 * inner)
        for i in range(kb):
            cross[i] += part((2 + i) * ncomp + u) * outer
    local = jnp.sum(local, axis=0, keepdims=True) / total
    local = local + pltpu.roll(local, width - THIRD, 1) + pltpu.roll(local, width - 2 * THIRD, 1)
    sums = lane_reduced(jnp.concatenate(over_cells(cross + [square]), axis=0)) / total
    proj = [local[0, i] - sums[0, i] for i in range(kb)]
    gram = [local[0, kb + 1 + i] for i in range(kb * kb)]

    def own(k):
        return own_ref[k, :, pl.ds(here, 1), :].reshape(ncomp, width)

    lane = lax.broadcasted_iota(jnp.int32, (ncomp, width), 1)
    edges = jnp.where(lane == 0, face_ref[0, :, 0, :], jnp.where(lane == width - 1, face_ref[1, :, 0, :], 0.0))
    outer = face_ref[2, :, 0, :] * own(0) + face_ref[3, :, 0, :] * own(1) + edges * own(2)
    finished(proj, gram, local[0, kb] + sums[0, kb], inner_ref[...] - outer, basis_ref, next_ref, hess_ref)


def one_exchange(before, after, panel_inverse, basis, jac_block, face_coef, rotor_offset):
    kb, ncomp, _, width = basis.shape
    theta_count = lax.axis_size("theta")
    band_count = lax.axis_size("band")
    devices = theta_count * band_count
    anywhere = pl.BlockSpec(memory_space=pl.ANY)
    *early, basis, face_coef, panel_inverse = pl.pallas_call(
        early_kernel,
        out_shape=(
            pltpu.VMEM(((2 + kb) * ncomp, width), jnp.float32),
            pltpu.VMEM((1, width), jnp.float32),
            pltpu.VMEM((ncomp, ncomp, width), jnp.float32),
            pltpu.VMEM(basis.shape, basis.dtype),
            pltpu.VMEM(face_coef.shape, face_coef.dtype),
            pltpu.VMEM(panel_inverse.shape, panel_inverse.dtype),
        ),
        in_specs=[anywhere] * 4,
        out_specs=specs(6),
        scratch_shapes=[pltpu.VMEM(jac_block.shape, jac_block.dtype), pltpu.SemaphoreType.DMA((4,))],
        name="early",
    )(basis, jac_block, face_coef, panel_inverse)
    send, inner, precond = pl.pallas_call(
        local_kernel,
        out_shape=(
            jax.ShapeDtypeStruct((devices * message_rows(kb, ncomp), width), jnp.bfloat16),
            pltpu.VMEM((ncomp, width), jnp.float32),
            jax.ShapeDtypeStruct((ncomp, 1, width), jnp.float32),
        ),
        in_specs=specs(8),
        out_specs=specs(3),
        name="local",
    )(*in_vmem(before, after, panel_inverse, basis, face_coef, *early))
    everyone = exchanged(send, devices)
    everyone = everyone.astype(jnp.float32)
    v_next, hess = pl.pallas_call(
        lambda *refs: merged_kernel(theta_count, band_count, *refs),
        out_shape=(
            jax.ShapeDtypeStruct((ncomp, 1, width), jnp.float32),
            jax.ShapeDtypeStruct((1, kb + 1), jnp.float32),
        ),
        in_specs=specs(4, 1),
        out_specs=specs(2),
        scratch_shapes=[pltpu.VMEM((3, ncomp, devices, width), jnp.float32)],
        name="merged",
    )(rotor_offset, *in_vmem(everyone, inner, basis, face_coef))
    return precond, v_next, hess


def exchanged(rows, devices):
    slots = rows.reshape(devices, -1, 2, rows.shape[-1])
    return lax.all_to_all(slots, AXES, 0, 0, tiled=True).reshape(rows.shape)


def on_device(basis, jac_block, face_coef, panel_inverse, rotor_offset):
    kb, ncomp, rows_here, width = basis.shape
    assert rows_here == 1
    half = width // 2
    theta_count = lax.axis_size("theta")
    band_count = lax.axis_size("band")
    up = [(i, (i + 1) % theta_count) for i in range(theta_count)]
    down = [(j, i) for i, j in up]
    before = lax.ppermute(basis, "theta", up)
    after = lax.ppermute(basis, "theta", down)
    if theta_count * band_count <= MERGED_LIMIT:
        precond, v_next, hess = one_exchange(before, after, panel_inverse, basis, jac_block, face_coef, rotor_offset)
        return precond, v_next, hess.reshape(kb + 1)
    before, current, after = (x[-1].astype(jnp.bfloat16) for x in (before, basis, after))
    extended = jnp.concatenate([before[..., half:], current, after[..., :half]], axis=2)
    panels = extended.reshape(ncomp, 2, width).transpose(1, 0, 2).reshape(2, ncomp * width)
    owned = jnp.einsum("pij,pj->pi", panel_inverse[0], panels, preferred_element_type=jnp.float32)
    precond = owned.reshape(2, ncomp, half).transpose(1, 0, 2).reshape(ncomp, 1, width)
    v_next, hess = two_exchanges(precond, basis, jac_block, face_coef, rotor_offset)
    return precond, v_next, hess.reshape(kb + 1)


def solution(mesh):
    return jax.shard_map(
        on_device,
        mesh=mesh,
        in_specs=(
            P(None, None, "band", "theta"),
            P(None, None, "band", "theta"),
            P(None, None, "band", "theta"),
            P("band", "theta", None, None),
            P(),
        ),
        out_specs=(P(None, "band", "theta"), P(None, "band", "theta"), P()),
        check_vma=False,
    )
```

```python
import jax
import jax.numpy as jnp
from jax import lax
from jax.experimental import pallas as pl
from jax.experimental.pallas import tpu as pltpu
from jax.sharding import PartitionSpec as P


AXES = ("theta", "band")
MERGED_LIMIT = 64
THIRD = 32


def even(count):
    return -(-count // 2) * 2


def in_vmem(*arrays):
    return [pltpu.with_memory_space_constraint(array, pltpu.VMEM) for array in arrays]


def specs(count, scalars=0):
    smem = pl.BlockSpec(memory_space=pltpu.SMEM)
    vmem = pl.BlockSpec(memory_space=pltpu.VMEM)
    return [smem] * scalars + [vmem] * count


def lane_reduced(rows):
    count, width = rows.shape
    sums = jnp.sum(rows, axis=1, keepdims=True)
    row = lax.broadcasted_iota(jnp.int32, (count, width), 0)
    lane = lax.broadcasted_iota(jnp.int32, (count, width), 1)
    return jnp.sum(jnp.where(row == lane, sums, 0.0), axis=0, keepdims=True)


def coupled(jac_ref, precond):
    out = jac_ref[:, 0, 0, :] * precond[0:1]
    for w in range(1, precond.shape[0]):
        out += jac_ref[:, w, 0, :] * precond[w : w + 1]
    return out


def over_cells(arrays):
    return [jnp.sum(array, axis=0, keepdims=True) for array in arrays]


def finished(proj, gram, square, image, basis_ref, next_ref, hess_ref):
    kb = basis_ref.shape[0]
    squares = square
    for i in range(kb):
        squares -= 2.0 * proj[i] * proj[i]
    for i in range(kb):
        for j in range(kb):
            squares += proj[i] * gram[i * kb + j] * proj[j]
    drop = proj[0] * basis_ref[0, :, 0, :]
    for i in range(1, kb):
        drop += proj[i] * basis_ref[i, :, 0, :]
    row = (1, image.shape[1])
    hnorm = jnp.sqrt(jnp.full(row, squares + 1e-06, jnp.float32))
    next_ref[:, 0, :] = (image - drop) / hnorm
    lane = lax.broadcasted_iota(jnp.int32, row, 1)
    hess = hnorm
    for i in range(kb):
        hess = jnp.where(lane == i, proj[i], hess)
    hess_ref[...] = hess[:, : kb + 1]


def image_kernel(theta_count, band_count, offset_ref, all_ref, basis_ref, jac_ref, face_ref, image_ref, send_ref):
    kb, ncomp, _, width = basis_ref.shape
    cycle = theta_count * width
    middle = band_count // 2
    theta = lax.axis_index("theta")
    band = lax.axis_index("band")
    offset = offset_ref[0]

    def cells_of(t, b):
        t = jnp.where(t >= theta_count, t - theta_count, t)
        return all_ref[t * band_count + b].reshape(ncomp, width)

    lane = lax.broadcasted_iota(jnp.int32, (ncomp, width), 1)

    def shifted(row, shift):
        start = theta * width + shift
        first = lax.rem(start // width, theta_count)
        skip = lax.rem(start, width)
        back = lax.rem(width - skip, width)
        one = pltpu.roll(cells_of(first, row), back, 1)
        two = pltpu.roll(cells_of(first + 1, row), back, 1)
        return jnp.where(lane < width - skip, one, two)

    precond = cells_of(theta, band)
    before = cells_of(theta + theta_count - 1, band)
    after = cells_of(theta + 1, band)
    theta_minus = jnp.where(lane == 0, pltpu.roll(before, 1, 1), pltpu.roll(precond, 1, 1))
    theta_plus = jnp.where(lane == width - 1, pltpu.roll(after, width - 1, 1), pltpu.roll(precond, width - 1, 1))
    up_shift = jnp.where(band == middle - 1, offset, 0)
    low_shift = jnp.where(band == middle, cycle - offset, 0)
    band_plus = shifted(jnp.minimum(band + 1, band_count - 1), up_shift)
    band_plus = jnp.where(band == band_count - 1, 0.0, band_plus)
    band_minus = shifted(jnp.maximum(band - 1, 0), low_shift)
    band_minus = jnp.where(band == 0, 0.0, band_minus)
    image = 6.0 * precond + coupled(jac_ref, precond)
    image = image - (
        face_ref[0, :, 0, :] * theta_minus
        + face_ref[1, :, 0, :] * theta_plus
        + face_ref[2, :, 0, :] * band_minus
        + face_ref[3, :, 0, :] * band_plus
    )
    image_ref[...] = image
    vectors = [basis_ref[i, :, 0, :] for i in range(kb)]
    pairs = [vectors[i] * image for i in range(kb)] + [image * image]
    pairs += [vectors[i] * vectors[j] for i in range(kb) for j in range(kb)]
    rows = jnp.concatenate(over_cells(pairs), axis=0)
    send_ref[...] = jnp.broadcast_to(lane_reduced(rows), send_ref.shape)


def finish_kernel(total, sums_ref, image_ref, basis_ref, next_ref, hess_ref):
    kb = basis_ref.shape[0]
    sums = jnp.sum(sums_ref[...], axis=0, keepdims=True) / total
    proj = [sums[0, i] for i in range(kb)]
    gram = [sums[0, kb + 1 + i] for i in range(kb * kb)]
    finished(proj, gram, sums[0, kb], image_ref[...], basis_ref, next_ref, hess_ref)


def two_exchanges(precond, basis, jac_block, face_coef, rotor_offset):
    kb, ncomp, _, width = basis.shape
    theta_count = lax.axis_size("theta")
    band_count = lax.axis_size("band")
    devices = theta_count * band_count
    copies = jnp.broadcast_to(precond[None], (devices, ncomp, 1, width))
    everyone = lax.all_to_all(copies, AXES, 0, 0, tiled=True)
    image, partial = pl.pallas_call(
        lambda *refs: image_kernel(theta_count, band_count, *refs),
        out_shape=(pltpu.VMEM((ncomp, width), jnp.float32), pltpu.VMEM((devices, width), jnp.float32)),
        in_specs=specs(4, 1),
        out_specs=specs(2),
        name="image",
    )(rotor_offset, *in_vmem(everyone, basis, jac_block, face_coef))
    sums = lax.all_to_all(partial, AXES, 0, 0, tiled=True)
    total = ncomp * devices * width
    return pl.pallas_call(
        lambda *refs: finish_kernel(total, *refs),
        out_shape=(
            jax.ShapeDtypeStruct((ncomp, 1, width), jnp.float32),
            jax.ShapeDtypeStruct((1, kb + 1), jnp.float32),
        ),
        in_specs=specs(3),
        out_specs=specs(2),
        name="finish",
    )(*in_vmem(sums, image, basis))


def thirds(x):
    high = x.astype(jnp.bfloat16).astype(jnp.float32)
    middle = (x - high).astype(jnp.bfloat16).astype(jnp.float32)
    return high, middle, x - high - middle


def message_rows(kb, ncomp):
    return even((4 + kb) * ncomp + 1)


def early_kernel(
    offset_ref, basis_hbm, jac_hbm, face_hbm, panel_hbm, static_ref, sums_ref, block_ref, basis_ref, face_ref, panel_ref, jac_ref, sems
):
    pairs = ((basis_hbm, basis_ref), (jac_hbm, jac_ref), (face_hbm, face_ref), (panel_hbm, panel_ref))
    copies = [pltpu.make_async_copy(source, target, sems.at[i]) for i, (source, target) in enumerate(pairs)]
    for copy in copies:
        copy.start()
    for copy in copies[:3]:
        copy.wait()
    kb, ncomp, _, width = basis_ref.shape
    vectors = [basis_ref[i, :, 0, :] for i in range(kb)]
    pairs = [vectors[i] * vectors[j] for i in range(kb) for j in range(kb)]
    blank = [jnp.zeros((1, width), jnp.float32)] * (kb + 1)
    rows = jnp.concatenate(blank + over_cells(pairs), axis=0)
    high, middle, low = thirds(lane_reduced(rows))
    sums = high + pltpu.roll(middle, THIRD, 1) + pltpu.roll(low, 2 * THIRD, 1)
    row = lax.broadcasted_iota(jnp.int32, (ncomp, width), 0)
    lane = lax.broadcasted_iota(jnp.int32, (ncomp, width), 1)
    first = jnp.where(lane == 3 * THIRD + row, face_ref[0, :, 0, :][:, :1], 0.0)
    last = jnp.where(lane == 3 * THIRD + THIRD // 2 + row, face_ref[1, :, 0, :][:, width - 1 :], 0.0)
    sums_ref[...] = sums + jnp.sum(first + last, axis=0, keepdims=True)
    static_ref[...] = jnp.concatenate([face_ref[2, :, 0, :], face_ref[3, :, 0, :], *vectors], axis=0)
    for w in range(ncomp):
        block_ref[w] = jac_ref[:, w, 0, :] + jnp.where(row == w, 6.0, 0.0)
    copies[3].wait()


def local_kernel(
    before_ref, after_ref, panel_ref, basis_ref, face_ref, static_ref, sums_ref, block_ref, send_ref, inner_ref, precond_ref
):
    kb, ncomp, _, width = basis_ref.shape
    half = width // 2
    slot = message_rows(kb, ncomp)
    lane = lax.broadcasted_iota(jnp.int32, (ncomp, width), 1)
    current = basis_ref[kb - 1, :, 0, :]
    swapped = pltpu.roll(current, half, 1)
    left = jnp.where(lane < half, pltpu.roll(before_ref[kb - 1, :, 0, :], half, 1), swapped)
    right = jnp.where(lane < half, swapped, pltpu.roll(after_ref[kb - 1, :, 0, :], half, 1))
    owned = []
    for h, cells in enumerate((left, right)):
        vector = jnp.concatenate([jnp.broadcast_to(cells[u : u + 1], (8, width)) for u in range(ncomp)], axis=1)
        owned.append(
            lax.dot_general(
                vector.astype(jnp.bfloat16),
                panel_ref[0, h],
                (((1,), (1,)), ((), ())),
                preferred_element_type=jnp.float32,
            )[:1]
        )
    halves = [[owned[h][:, u * half : (u + 1) * half] for u in range(ncomp)] for h in range(2)]
    precond = jnp.concatenate([jnp.concatenate([halves[0][u], halves[1][u]], axis=1) for u in range(ncomp)], axis=0)
    precond_ref[...] = precond
    lower = jnp.where(lane == 0, 0.0, pltpu.roll(precond, 1, 1))
    upper = jnp.where(lane == width - 1, 0.0, pltpu.roll(precond, width - 1, 1))
    inner = block_ref[0] * precond[0:1]
    for w in range(1, ncomp):
        inner += block_ref[w] * precond[w : w + 1]
    inner = inner - (face_ref[0, :, 0, :] * lower + face_ref[1, :, 0, :] * upper)
    inner_ref[...] = inner
    pairs = [basis_ref[i, :, 0, :] * inner for i in range(kb)] + [inner * inner]
    high, middle, low = thirds(lane_reduced(jnp.concatenate(over_cells(pairs), axis=0)))
    sums = sums_ref[...] + high + pltpu.roll(middle, THIRD, 1) + pltpu.roll(low, 2 * THIRD, 1)
    groups = [static_ref[...], inner, precond, sums]
    if slot > (4 + kb) * ncomp + 1:
        groups.append(jnp.zeros((slot - (4 + kb) * ncomp - 1, width), jnp.float32))
    message = jnp.concatenate(groups, axis=0).astype(jnp.bfloat16)
    for device in range(send_ref.shape[0] // slot):
        send_ref[device * slot : (device + 1) * slot] = message


def merged_kernel(theta_count, band_count, offset_ref, all_ref, inner_ref, precond_ref, basis_ref, face_ref, out_ref, next_ref, hess_ref, own_ref):
    kb, ncomp, _, width = basis_ref.shape
    out_ref[:, 0, :] = precond_ref[...]
    devices = theta_count * band_count
    cycle = theta_count * width
    total = ncomp * devices * width
    middle = band_count // 2
    shape = (devices, width)
    row = lax.broadcasted_iota(jnp.int32, shape, 0)
    lane = lax.broadcasted_iota(jnp.int32, shape, 1)
    band = lax.rem(row, band_count)
    here = lax.axis_index("theta") * band_count + lax.axis_index("band")
    base = cycle // 2 - width
    start = offset_ref[0] - base
    late = start >= width
    skip = jnp.where(late, start - width, start)

    def part(place):
        return all_ref[pl.ds(place, devices, stride=all_ref.shape[0] // devices), :]

    def rows_up(x, count):
        return pltpu.roll(x, (devices - count) % devices, 0)

    half = theta_count // 2
    local = part((4 + kb) * ncomp)
    square = jnp.zeros(shape, jnp.float32)
    cross = [jnp.zeros(shape, jnp.float32) for _ in range(kb)]
    for u in range(ncomp):
        inner, precond = part((2 + kb) * ncomp + u), part((3 + kb) * ncomp + u)
        turned = pltpu.roll(precond, lax.rem(width - skip, width), 1)
        near, at, far = (rows_up(turned, (half + k) * band_count + 1) for k in (-1, 0, 1))
        split = lane < width - skip
        rotor_up = jnp.where(split, jnp.where(late, at, near), jnp.where(late, far, at))
        turned = pltpu.roll(precond, skip, 1)
        near, at, far = (rows_up(turned, (-half + k) * band_count - 1) for k in (1, 0, -1))
        split = lane >= skip
        rotor_down = jnp.where(split, jnp.where(late, at, near), jnp.where(late, far, at))
        band_plus = jnp.where(band == middle - 1, rotor_up, rows_up(precond, 1))
        band_plus = jnp.where(band == band_count - 1, 0.0, band_plus)
        band_minus = jnp.where(band == middle, rotor_down, rows_up(precond, -1))
        band_minus = jnp.where(band == 0, 0.0, band_minus)
        before = rows_up(pltpu.roll(precond, 1, 1), -band_count)
        after = rows_up(pltpu.roll(precond, width - 1, 1), band_count)
        edge = jnp.where(lane == 0, before, after)
        place = 3 * THIRD + u
        first = pltpu.roll(local, width - place, 1)
        last = pltpu.roll(local, width - 1 - place - THIRD // 2, 1)
        coef = jnp.where(lane == 0, first, jnp.where(lane == width - 1, last, 0.0))
        own_ref[0, u] = band_minus
        own_ref[1, u] = band_plus
        own_ref[2, u] = edge
        outer = part(u) * band_minus + part(ncomp + u) * band_plus + coef * edge
        square += outer * (outer - 2.0 * inner)
        for i in range(kb):
            cross[i] += part((2 + i) * ncomp + u) * outer
    local = jnp.sum(local, axis=0, keepdims=True) / total
    local = local + pltpu.roll(local, width - THIRD, 1) + pltpu.roll(local, width - 2 * THIRD, 1)
    sums = lane_reduced(jnp.concatenate(over_cells(cross + [square]), axis=0)) / total
    proj = [local[0, i] - sums[0, i] for i in range(kb)]
    gram = [local[0, kb + 1 + i] for i in range(kb * kb)]

    def own(k):
        return own_ref[k, :, pl.ds(here, 1), :].reshape(ncomp, width)

    lane = lax.broadcasted_iota(jnp.int32, (ncomp, width), 1)
    edges = jnp.where(lane == 0, face_ref[0, :, 0, :], jnp.where(lane == width - 1, face_ref[1, :, 0, :], 0.0))
    outer = face_ref[2, :, 0, :] * own(0) + face_ref[3, :, 0, :] * own(1) + edges * own(2)
    finished(proj, gram, local[0, kb] + sums[0, kb], inner_ref[...] - outer, basis_ref, next_ref, hess_ref)


def one_exchange(before, after, panel_inverse, basis, jac_block, face_coef, rotor_offset):
    kb, ncomp, _, width = basis.shape
    theta_count = lax.axis_size("theta")
    band_count = lax.axis_size("band")
    devices = theta_count * band_count
    anywhere = pl.BlockSpec(memory_space=pl.ANY)
    *early, basis, face_coef, panel_inverse = pl.pallas_call(
        early_kernel,
        out_shape=(
            pltpu.VMEM(((2 + kb) * ncomp, width), jnp.float32),
            pltpu.VMEM((1, width), jnp.float32),
            pltpu.VMEM((ncomp, ncomp, width), jnp.float32),
            pltpu.VMEM(basis.shape, basis.dtype),
            pltpu.VMEM(face_coef.shape, face_coef.dtype),
            pltpu.VMEM(panel_inverse.shape, panel_inverse.dtype),
        ),
        in_specs=specs(0, 1) + [anywhere] * 4,
        out_specs=specs(6),
        scratch_shapes=[pltpu.VMEM(jac_block.shape, jac_block.dtype), pltpu.SemaphoreType.DMA((4,))],
        name="early",
    )(rotor_offset, basis, jac_block, face_coef, panel_inverse)
    send, inner, precond = pl.pallas_call(
        local_kernel,
        out_shape=(
            pltpu.VMEM((devices * message_rows(kb, ncomp), width), jnp.bfloat16),
            pltpu.VMEM((ncomp, width), jnp.float32),
            pltpu.VMEM((ncomp, width), jnp.float32),
        ),
        in_specs=specs(8),
        out_specs=specs(3),
        name="local",
    )(*in_vmem(before, after, panel_inverse, basis, face_coef, *early))
    everyone = exchanged(send, devices)
    everyone = everyone.astype(jnp.float32)
    return pl.pallas_call(
        lambda *refs: merged_kernel(theta_count, band_count, *refs),
        out_shape=(
            jax.ShapeDtypeStruct((ncomp, 1, width), jnp.float32),
            jax.ShapeDtypeStruct((ncomp, 1, width), jnp.float32),
            jax.ShapeDtypeStruct((1, kb + 1), jnp.float32),
        ),
        in_specs=specs(5, 1),
        out_specs=specs(3),
        scratch_shapes=[pltpu.VMEM((3, ncomp, devices, width), jnp.float32)],
        name="merged",
    )(rotor_offset, *in_vmem(everyone, inner, precond, basis, face_coef))


def exchanged(rows, devices):
    slots = rows.reshape(devices, -1, 2, rows.shape[-1])
    return lax.all_to_all(slots, AXES, 0, 0, tiled=True).reshape(rows.shape)


def on_device(basis, jac_block, face_coef, panel_inverse, rotor_offset):
    kb, ncomp, rows_here, width = basis.shape
    assert rows_here == 1
    half = width // 2
    theta_count = lax.axis_size("theta")
    band_count = lax.axis_size("band")
    up = [(i, (i + 1) % theta_count) for i in range(theta_count)]
    down = [(j, i) for i, j in up]
    before = lax.ppermute(basis, "theta", up)
    after = lax.ppermute(basis, "theta", down)
    if theta_count * band_count <= MERGED_LIMIT:
        precond, v_next, hess = one_exchange(before, after, panel_inverse, basis, jac_block, face_coef, rotor_offset)
        return precond, v_next, hess.reshape(kb + 1)
    before, current, after = (x[-1].astype(jnp.bfloat16) for x in (before, basis, after))
    extended = jnp.concatenate([before[..., half:], current, after[..., :half]], axis=2)
    panels = extended.reshape(ncomp, 2, width).transpose(1, 0, 2).reshape(2, ncomp * width)
    owned = jnp.einsum("pij,pj->pi", panel_inverse[0], panels, preferred_element_type=jnp.float32)
    precond = owned.reshape(2, ncomp, half).transpose(1, 0, 2).reshape(ncomp, 1, width)
    v_next, hess = two_exchanges(precond, basis, jac_block, face_coef, rotor_offset)
    return precond, v_next, hess.reshape(kb + 1)


def solution(mesh):
    return jax.shard_map(
        on_device,
        mesh=mesh,
        in_specs=(
            P(None, None, "band", "theta"),
            P(None, None, "band", "theta"),
            P(None, None, "band", "theta"),
            P("band", "theta", None, None),
            P(),
        ),
        out_specs=(P(None, "band", "theta"), P(None, "band", "theta"), P()),
        check_vma=False,
    )
```

```python
import jax
import jax.numpy as jnp
from jax import lax
from jax.experimental import pallas as pl
from jax.experimental.pallas import tpu as pltpu
from jax.sharding import PartitionSpec as P


AXES = ("theta", "band")
MERGED_LIMIT = 64
THIRD = 32
EIGHT = 8


def even(count):
    return -(-count // 2) * 2


def in_vmem(*arrays):
    return [pltpu.with_memory_space_constraint(array, pltpu.VMEM) for array in arrays]


def specs(count, scalars=0):
    smem = pl.BlockSpec(memory_space=pltpu.SMEM)
    vmem = pl.BlockSpec(memory_space=pltpu.VMEM)
    return [smem] * scalars + [vmem] * count


def lane_reduced(rows):
    count, width = rows.shape
    sums = jnp.sum(rows, axis=1, keepdims=True)
    row = lax.broadcasted_iota(jnp.int32, (count, width), 0)
    lane = lax.broadcasted_iota(jnp.int32, (count, width), 1)
    return jnp.sum(jnp.where(row == lane, sums, 0.0), axis=0, keepdims=True)


def coupled(jac_ref, precond):
    out = jac_ref[:, 0, 0, :] * precond[0:1]
    for w in range(1, precond.shape[0]):
        out += jac_ref[:, w, 0, :] * precond[w : w + 1]
    return out


def over_cells(arrays):
    return [jnp.sum(array, axis=0, keepdims=True) for array in arrays]


def finished(proj, gram, square, image, basis_ref, next_ref, hess_ref):
    kb = basis_ref.shape[0]
    squares = square
    for i in range(kb):
        squares -= 2.0 * proj[i] * proj[i]
    for i in range(kb):
        for j in range(kb):
            squares += proj[i] * gram[i * kb + j] * proj[j]
    drop = proj[0] * basis_ref[0, :, 0, :]
    for i in range(1, kb):
        drop += proj[i] * basis_ref[i, :, 0, :]
    row = (1, image.shape[1])
    hnorm = jnp.sqrt(jnp.full(row, squares + 1e-06, jnp.float32))
    next_ref[:, 0, :] = (image - drop) / hnorm
    lane = lax.broadcasted_iota(jnp.int32, row, 1)
    hess = hnorm
    for i in range(kb):
        hess = jnp.where(lane == i, proj[i], hess)
    hess_ref[...] = hess[:, : kb + 1]


def image_kernel(theta_count, band_count, offset_ref, all_ref, basis_ref, jac_ref, face_ref, image_ref, send_ref):
    kb, ncomp, _, width = basis_ref.shape
    cycle = theta_count * width
    middle = band_count // 2
    theta = lax.axis_index("theta")
    band = lax.axis_index("band")
    offset = offset_ref[0]

    def cells_of(t, b):
        t = jnp.where(t >= theta_count, t - theta_count, t)
        return all_ref[t * band_count + b].reshape(ncomp, width)

    lane = lax.broadcasted_iota(jnp.int32, (ncomp, width), 1)

    def shifted(row, shift):
        start = theta * width + shift
        first = lax.rem(start // width, theta_count)
        skip = lax.rem(start, width)
        back = lax.rem(width - skip, width)
        one = pltpu.roll(cells_of(first, row), back, 1)
        two = pltpu.roll(cells_of(first + 1, row), back, 1)
        return jnp.where(lane < width - skip, one, two)

    precond = cells_of(theta, band)
    before = cells_of(theta + theta_count - 1, band)
    after = cells_of(theta + 1, band)
    theta_minus = jnp.where(lane == 0, pltpu.roll(before, 1, 1), pltpu.roll(precond, 1, 1))
    theta_plus = jnp.where(lane == width - 1, pltpu.roll(after, width - 1, 1), pltpu.roll(precond, width - 1, 1))
    up_shift = jnp.where(band == middle - 1, offset, 0)
    low_shift = jnp.where(band == middle, cycle - offset, 0)
    band_plus = shifted(jnp.minimum(band + 1, band_count - 1), up_shift)
    band_plus = jnp.where(band == band_count - 1, 0.0, band_plus)
    band_minus = shifted(jnp.maximum(band - 1, 0), low_shift)
    band_minus = jnp.where(band == 0, 0.0, band_minus)
    image = 6.0 * precond + coupled(jac_ref, precond)
    image = image - (
        face_ref[0, :, 0, :] * theta_minus
        + face_ref[1, :, 0, :] * theta_plus
        + face_ref[2, :, 0, :] * band_minus
        + face_ref[3, :, 0, :] * band_plus
    )
    image_ref[...] = image
    vectors = [basis_ref[i, :, 0, :] for i in range(kb)]
    pairs = [vectors[i] * image for i in range(kb)] + [image * image]
    pairs += [vectors[i] * vectors[j] for i in range(kb) for j in range(kb)]
    rows = jnp.concatenate(over_cells(pairs), axis=0)
    send_ref[...] = jnp.broadcast_to(lane_reduced(rows), send_ref.shape)


def finish_kernel(total, sums_ref, image_ref, basis_ref, next_ref, hess_ref):
    kb = basis_ref.shape[0]
    sums = jnp.sum(sums_ref[...], axis=0, keepdims=True) / total
    proj = [sums[0, i] for i in range(kb)]
    gram = [sums[0, kb + 1 + i] for i in range(kb * kb)]
    finished(proj, gram, sums[0, kb], image_ref[...], basis_ref, next_ref, hess_ref)


def two_exchanges(precond, basis, jac_block, face_coef, rotor_offset):
    kb, ncomp, _, width = basis.shape
    theta_count = lax.axis_size("theta")
    band_count = lax.axis_size("band")
    devices = theta_count * band_count
    copies = jnp.broadcast_to(precond[None], (devices, ncomp, 1, width))
    everyone = lax.all_to_all(copies, AXES, 0, 0, tiled=True)
    image, partial = pl.pallas_call(
        lambda *refs: image_kernel(theta_count, band_count, *refs),
        out_shape=(pltpu.VMEM((ncomp, width), jnp.float32), pltpu.VMEM((devices, width), jnp.float32)),
        in_specs=specs(4, 1),
        out_specs=specs(2),
        name="image",
    )(rotor_offset, *in_vmem(everyone, basis, jac_block, face_coef))
    sums = lax.all_to_all(partial, AXES, 0, 0, tiled=True)
    total = ncomp * devices * width
    return pl.pallas_call(
        lambda *refs: finish_kernel(total, *refs),
        out_shape=(
            jax.ShapeDtypeStruct((ncomp, 1, width), jnp.float32),
            jax.ShapeDtypeStruct((1, kb + 1), jnp.float32),
        ),
        in_specs=specs(3),
        out_specs=specs(2),
        name="finish",
    )(*in_vmem(sums, image, basis))


def thirds(x):
    high = x.astype(jnp.bfloat16).astype(jnp.float32)
    middle = (x - high).astype(jnp.bfloat16).astype(jnp.float32)
    return high, middle, x - high - middle


def shared_pairs(kb, ncomp):
    pairs = [(i, u) for i in range(kb) for u in range(ncomp)]
    count = -(-(kb + 1) * ncomp // 2)
    return pairs[:count], pairs[count:]


def message_rows(kb, ncomp):
    return even(3 * ncomp + 2 + len(shared_pairs(kb, ncomp)[0]))


def places(base, array):
    row = lax.broadcasted_iota(jnp.int32, array.shape, 0)
    lane = lax.broadcasted_iota(jnp.int32, array.shape, 1)
    width = array.shape[1]
    out = jnp.where(lane == base + row, array[:, :1], 0.0)
    return out + jnp.where(lane == base + width // 2 + row, array[:, width - 1 :], 0.0)


def early_kernel(
    basis_hbm, jac_hbm, face_hbm, panel_hbm, offset_hbm, sums_ref, edge_ref, block_ref, basis_ref, face_ref, panel_ref, offset_ref, jac_ref, sems
):
    pairs = ((basis_hbm, basis_ref), (jac_hbm, jac_ref), (face_hbm, face_ref), (panel_hbm, panel_ref), (offset_hbm, offset_ref))
    copies = [pltpu.make_async_copy(source, target, sems.at[i]) for i, (source, target) in enumerate(pairs)]
    for copy in copies:
        copy.start()
    for copy in copies[:3]:
        copy.wait()
    kb, ncomp, _, width = basis_ref.shape
    vectors = [basis_ref[i, :, 0, :] for i in range(kb)]
    pairs = [vectors[i] * vectors[j] for i in range(kb) for j in range(kb)]
    blank = [jnp.zeros((1, width), jnp.float32)] * (kb + 1)
    rows = jnp.concatenate(blank + over_cells(pairs), axis=0)
    high, middle, low = thirds(lane_reduced(rows))
    sums_ref[...] = high + pltpu.roll(middle, THIRD, 1) + pltpu.roll(low, 2 * THIRD, 1)
    row = lax.broadcasted_iota(jnp.int32, (ncomp, width), 0)
    lane = lax.broadcasted_iota(jnp.int32, (ncomp, width), 1)
    edges = jnp.where(lane < width // 2, face_ref[0, :, 0, :], face_ref[1, :, 0, :])
    edge = sum(places(EIGHT * i, array) for i, array in enumerate([edges, *vectors]))
    edge_ref[...] = jnp.sum(edge, axis=0, keepdims=True)
    for w in range(ncomp):
        block_ref[w] = jac_ref[:, w, 0, :] + jnp.where(row == w, 6.0, 0.0)
    copies[3].wait()
    copies[4].wait()


def local_kernel(
    before_ref,
    after_ref,
    far_basis_ref,
    far_face_ref,
    panel_ref,
    basis_ref,
    face_ref,
    sums_ref,
    edge_ref,
    block_ref,
    send_ref,
    inner_ref,
    precond_ref,
):
    kb, ncomp, _, width = basis_ref.shape
    half = width // 2
    slot = message_rows(kb, ncomp)
    lane = lax.broadcasted_iota(jnp.int32, (ncomp, width), 1)
    current = basis_ref[kb - 1, :, 0, :]
    swapped = pltpu.roll(current, half, 1)
    left = jnp.where(lane < half, pltpu.roll(before_ref[kb - 1, :, 0, :], half, 1), swapped)
    right = jnp.where(lane < half, swapped, pltpu.roll(after_ref[kb - 1, :, 0, :], half, 1))
    owned = []
    for h, cells in enumerate((left, right)):
        vector = jnp.concatenate([jnp.broadcast_to(cells[u : u + 1], (8, width)) for u in range(ncomp)], axis=1)
        owned.append(
            lax.dot_general(
                vector.astype(jnp.bfloat16),
                panel_ref[0, h],
                (((1,), (1,)), ((), ())),
                preferred_element_type=jnp.float32,
            )[:1]
        )
    halves = [[owned[h][:, u * half : (u + 1) * half] for u in range(ncomp)] for h in range(2)]
    precond = jnp.concatenate([jnp.concatenate([halves[0][u], halves[1][u]], axis=1) for u in range(ncomp)], axis=0)
    precond_ref[...] = precond
    lower = jnp.where(lane == 0, 0.0, pltpu.roll(precond, 1, 1))
    upper = jnp.where(lane == width - 1, 0.0, pltpu.roll(precond, width - 1, 1))
    inner = block_ref[0] * precond[0:1]
    for w in range(1, ncomp):
        inner += block_ref[w] * precond[w : w + 1]
    inner = inner - (face_ref[0, :, 0, :] * lower + face_ref[1, :, 0, :] * upper)
    inner_ref[...] = inner
    band = lax.axis_index("band")
    is_even = lax.rem(band, 2) == 0
    beside = jnp.logical_or(band == 1, band == 2)
    lower_face, upper_face = face_ref[2, :, 0, :], face_ref[3, :, 0, :]
    to_partner = jnp.where(is_even, upper_face, lower_face)
    to_rotor = jnp.where(is_even, lower_face, upper_face)
    reach = jnp.where(is_even, far_face_ref[2, :, 0, :], far_face_ref[3, :, 0, :]) * precond
    pairs = [basis_ref[i, :, 0, :] * inner - far_basis_ref[i, :, 0, :] * reach for i in range(kb)] + [inner * inner]
    high, middle, low = thirds(lane_reduced(jnp.concatenate(over_cells(pairs), axis=0)))
    sums = sums_ref[...] + high + pltpu.roll(middle, THIRD, 1) + pltpu.roll(low, 2 * THIRD, 1)
    carried, kept = shared_pairs(kb, ncomp)
    for_partner = jnp.concatenate([far_basis_ref[i, u : u + 1, 0, :] for i, u in carried], axis=0)
    spare = [jnp.zeros((1, width), jnp.float32)] * (len(carried) - ncomp - len(kept))
    own_part = jnp.concatenate([to_rotor] + [basis_ref[i, u : u + 1, 0, :] for i, u in kept] + spare, axis=0)
    groups = [to_partner, inner, precond, sums, edge_ref[...], jnp.where(beside, own_part, for_partner)]
    filled = 3 * ncomp + 2 + len(carried)
    if slot > filled:
        groups.append(jnp.zeros((slot - filled, width), jnp.float32))
    message = jnp.concatenate(groups, axis=0).astype(jnp.bfloat16)
    for device in range(send_ref.shape[0] // slot):
        send_ref[device * slot : (device + 1) * slot] = message


def merged_kernel(theta_count, band_count, offset_ref, all_ref, inner_ref, precond_ref, basis_ref, face_ref, out_ref, next_ref, hess_ref, own_ref):
    kb, ncomp, _, width = basis_ref.shape
    out_ref[:, 0, :] = precond_ref[...]
    devices = theta_count * band_count
    cycle = theta_count * width
    total = ncomp * devices * width
    middle = band_count // 2
    shape = (devices, width)
    row = lax.broadcasted_iota(jnp.int32, shape, 0)
    lane = lax.broadcasted_iota(jnp.int32, shape, 1)
    band = lax.rem(row, band_count)
    here = lax.axis_index("theta") * band_count + lax.axis_index("band")
    base = cycle // 2 - width
    start = offset_ref[0] - base
    late = start >= width
    skip = jnp.where(late, start - width, start)

    def part(place):
        return all_ref[pl.ds(place, devices, stride=all_ref.shape[0] // devices), :]

    def rows_up(x, count):
        return pltpu.roll(x, (devices - count) % devices, 0)

    half = theta_count // 2
    is_even = lax.rem(band, 2) == 0
    beside = jnp.logical_or(band == middle - 1, band == middle)
    local, edge_row = part(3 * ncomp), part(3 * ncomp + 1)
    tail = 3 * ncomp + 2
    square = jnp.zeros(shape, jnp.float32)
    at_edges = jnp.zeros(shape, jnp.float32)
    turns, handed = [], []
    for u in range(ncomp):
        inner, precond = part(ncomp + u), part(2 * ncomp + u)
        turned = pltpu.roll(precond, lax.rem(width - skip, width), 1)
        near, at, far = (rows_up(turned, (half + k) * band_count + 1) for k in (-1, 0, 1))
        split = lane < width - skip
        rotor_up = jnp.where(split, jnp.where(late, at, near), jnp.where(late, far, at))
        turned = pltpu.roll(precond, skip, 1)
        near, at, far = (rows_up(turned, (-half + k) * band_count - 1) for k in (1, 0, -1))
        split = lane >= skip
        rotor_down = jnp.where(split, jnp.where(late, at, near), jnp.where(late, far, at))
        rotor = jnp.where(band == middle - 1, rotor_up, jnp.where(band == middle, rotor_down, 0.0))
        partner = jnp.where(is_even, rows_up(precond, 1), rows_up(precond, -1))
        before = rows_up(pltpu.roll(precond, 1, 1), -band_count)
        after = rows_up(pltpu.roll(precond, width - 1, 1), band_count)
        edge = jnp.where(lane == 0, before, after)
        first = pltpu.roll(edge_row, (width - u) % width, 1)
        last = pltpu.roll(edge_row, width - 1 - width // 2 - u, 1)
        coef = jnp.where(lane == 0, first, jnp.where(lane == width - 1, last, 0.0))
        own_ref[0, u] = partner
        own_ref[1, u] = rotor
        own_ref[2, u] = edge
        rim = coef * edge
        turn = part(tail + u) * rotor
        turns.append(turn)
        handed.append(jnp.where(is_even, rows_up(turn, 1), rows_up(turn, -1)))
        outer = part(u) * partner + turn + rim
        square += outer * (outer - 2.0 * inner)
        at_edges = jnp.where(lane == u, pltpu.roll(rim, u, 1), at_edges)
        at_edges = jnp.where(lane == width // 2 + u, pltpu.roll(rim, width // 2 + 1 + u, 1), at_edges)
    carried, kept = shared_pairs(kb, ncomp)
    cross = [pltpu.roll(edge_row, width - EIGHT * (i + 1), 1) * at_edges for i in range(kb)]
    in_partner = [jnp.zeros(shape, jnp.float32) for _ in range(kb)]
    in_own = [jnp.zeros(shape, jnp.float32) for _ in range(kb)]
    for place, (i, u) in enumerate(carried):
        values = handed[u]
        mine = place - ncomp
        if 0 <= mine < len(kept):
            values = jnp.where(beside, turns[kept[mine][1]], values)
        product = part(tail + place) * values
        in_partner[i] += product
        if 0 <= mine < len(kept):
            in_own[kept[mine][0]] += product
    cross = [cross[i] + jnp.where(beside, in_own[i], in_partner[i]) for i in range(kb)]
    local = jnp.sum(local, axis=0, keepdims=True) / total
    local = local + pltpu.roll(local, width - THIRD, 1) + pltpu.roll(local, width - 2 * THIRD, 1)
    sums = lane_reduced(jnp.concatenate(over_cells(cross + [square]), axis=0)) / total
    proj = [local[0, i] - sums[0, i] for i in range(kb)]
    gram = [local[0, kb + 1 + i] for i in range(kb * kb)]

    def own(k):
        return own_ref[k, :, pl.ds(here, 1), :].reshape(ncomp, width)

    lane = lax.broadcasted_iota(jnp.int32, (ncomp, width), 1)
    edges = jnp.where(lane == 0, face_ref[0, :, 0, :], jnp.where(lane == width - 1, face_ref[1, :, 0, :], 0.0))
    is_even = lax.rem(lax.axis_index("band"), 2) == 0
    lower_face, upper_face = face_ref[2, :, 0, :], face_ref[3, :, 0, :]
    outer = jnp.where(is_even, upper_face, lower_face) * own(0) + edges * own(2)
    outer += jnp.where(is_even, lower_face, upper_face) * own(1)
    finished(proj, gram, local[0, kb] + sums[0, kb], inner_ref[...] - outer, basis_ref, next_ref, hess_ref)


def one_exchange(before, after, far, panel_inverse, basis, jac_block, face_coef, rotor_offset):
    kb, ncomp, _, width = basis.shape
    theta_count = lax.axis_size("theta")
    band_count = lax.axis_size("band")
    devices = theta_count * band_count
    anywhere = pl.BlockSpec(memory_space=pl.ANY)
    *early, basis, face_coef, panel_inverse, rotor_offset = pl.pallas_call(
        early_kernel,
        out_shape=(
            pltpu.VMEM((1, width), jnp.float32),
            pltpu.VMEM((1, width), jnp.float32),
            pltpu.VMEM((ncomp, ncomp, width), jnp.float32),
            pltpu.VMEM(basis.shape, basis.dtype),
            pltpu.VMEM(face_coef.shape, face_coef.dtype),
            pltpu.VMEM(panel_inverse.shape, panel_inverse.dtype),
            pltpu.SMEM(rotor_offset.shape, rotor_offset.dtype),
        ),
        in_specs=[anywhere] * 5,
        out_specs=specs(6) + specs(0, 1),
        scratch_shapes=[pltpu.VMEM(jac_block.shape, jac_block.dtype), pltpu.SemaphoreType.DMA((5,))],
        name="early",
    )(basis, jac_block, face_coef, panel_inverse, rotor_offset)
    send, inner, precond = pl.pallas_call(
        local_kernel,
        out_shape=(
            pltpu.VMEM((devices * message_rows(kb, ncomp), width), jnp.bfloat16),
            pltpu.VMEM((ncomp, width), jnp.float32),
            pltpu.VMEM((ncomp, width), jnp.float32),
        ),
        in_specs=specs(10),
        out_specs=specs(3),
        name="local",
    )(*in_vmem(before, after, *far, panel_inverse, basis, face_coef, *early))
    everyone = exchanged(send, devices)
    everyone = everyone.astype(jnp.float32)
    return pl.pallas_call(
        lambda *refs: merged_kernel(theta_count, band_count, *refs),
        out_shape=(
            jax.ShapeDtypeStruct((ncomp, 1, width), jnp.float32),
            jax.ShapeDtypeStruct((ncomp, 1, width), jnp.float32),
            jax.ShapeDtypeStruct((1, kb + 1), jnp.float32),
        ),
        in_specs=specs(5, 1),
        out_specs=specs(3),
        scratch_shapes=[pltpu.VMEM((3, ncomp, devices, width), jnp.float32)],
        name="merged",
    )(rotor_offset, *in_vmem(everyone, inner, precond, basis, face_coef))


def exchanged(rows, devices):
    slots = rows.reshape(devices, -1, 2, rows.shape[-1])
    return lax.all_to_all(slots, AXES, 0, 0, tiled=True).reshape(rows.shape)


def on_device(basis, jac_block, face_coef, panel_inverse, rotor_offset):
    kb, ncomp, rows_here, width = basis.shape
    assert rows_here == 1
    half = width // 2
    theta_count = lax.axis_size("theta")
    band_count = lax.axis_size("band")
    up = [(i, (i + 1) % theta_count) for i in range(theta_count)]
    down = [(j, i) for i, j in up]
    before = lax.ppermute(basis, "theta", up)
    after = lax.ppermute(basis, "theta", down)
    if theta_count * band_count <= MERGED_LIMIT and band_count == 4:
        pairs = [(b, b + 1 - 2 * (b % 2)) for b in range(band_count)]
        far_basis = lax.ppermute(basis, "band", pairs)
        far = [far_basis, lax.ppermute(face_coef, "band", pairs)]
        precond, v_next, hess = one_exchange(before, after, far, panel_inverse, basis, jac_block, face_coef, rotor_offset)
        return precond, v_next, hess.reshape(kb + 1)
    before, current, after = (x[-1].astype(jnp.bfloat16) for x in (before, basis, after))
    extended = jnp.concatenate([before[..., half:], current, after[..., :half]], axis=2)
    panels = extended.reshape(ncomp, 2, width).transpose(1, 0, 2).reshape(2, ncomp * width)
    owned = jnp.einsum("pij,pj->pi", panel_inverse[0], panels, preferred_element_type=jnp.float32)
    precond = owned.reshape(2, ncomp, half).transpose(1, 0, 2).reshape(ncomp, 1, width)
    v_next, hess = two_exchanges(precond, basis, jac_block, face_coef, rotor_offset)
    return precond, v_next, hess.reshape(kb + 1)


def solution(mesh):
    return jax.shard_map(
        on_device,
        mesh=mesh,
        in_specs=(
            P(None, None, "band", "theta"),
            P(None, None, "band", "theta"),
            P(None, None, "band", "theta"),
            P("band", "theta", None, None),
            P(),
        ),
        out_specs=(P(None, "band", "theta"), P(None, "band", "theta"), P()),
        check_vma=False,
    )
```

```python
import jax
import jax.numpy as jnp
from jax import lax
from jax.experimental import pallas as pl
from jax.experimental.pallas import tpu as pltpu
from jax.sharding import PartitionSpec as P


AXES = ("theta", "band")
MERGED_LIMIT = 64
THIRD = 32
EIGHT = 8


def even(count):
    return -(-count // 2) * 2


def in_vmem(*arrays):
    return [pltpu.with_memory_space_constraint(array, pltpu.VMEM) for array in arrays]


def specs(count, scalars=0):
    smem = pl.BlockSpec(memory_space=pltpu.SMEM)
    vmem = pl.BlockSpec(memory_space=pltpu.VMEM)
    return [smem] * scalars + [vmem] * count


def lane_reduced(rows):
    count, width = rows.shape
    sums = jnp.sum(rows, axis=1, keepdims=True)
    row = lax.broadcasted_iota(jnp.int32, (count, width), 0)
    lane = lax.broadcasted_iota(jnp.int32, (count, width), 1)
    return jnp.sum(jnp.where(row == lane, sums, 0.0), axis=0, keepdims=True)


def coupled(jac_ref, precond):
    out = jac_ref[:, 0, 0, :] * precond[0:1]
    for w in range(1, precond.shape[0]):
        out += jac_ref[:, w, 0, :] * precond[w : w + 1]
    return out


def over_cells(arrays):
    return [jnp.sum(array, axis=0, keepdims=True) for array in arrays]


def finished(proj, gram, square, image, basis_ref, next_ref, hess_ref):
    kb = basis_ref.shape[0]
    squares = square
    for i in range(kb):
        squares -= 2.0 * proj[i] * proj[i]
    for i in range(kb):
        for j in range(kb):
            squares += proj[i] * gram[i * kb + j] * proj[j]
    drop = proj[0] * basis_ref[0, :, 0, :]
    for i in range(1, kb):
        drop += proj[i] * basis_ref[i, :, 0, :]
    row = (1, image.shape[1])
    hnorm = jnp.sqrt(jnp.full(row, squares + 1e-06, jnp.float32))
    next_ref[:, 0, :] = (image - drop) / hnorm
    lane = lax.broadcasted_iota(jnp.int32, row, 1)
    hess = hnorm
    for i in range(kb):
        hess = jnp.where(lane == i, proj[i], hess)
    hess_ref[...] = hess[:, : kb + 1]


def image_kernel(theta_count, band_count, offset_ref, all_ref, basis_ref, jac_ref, face_ref, image_ref, send_ref):
    kb, ncomp, _, width = basis_ref.shape
    cycle = theta_count * width
    middle = band_count // 2
    theta = lax.axis_index("theta")
    band = lax.axis_index("band")
    offset = offset_ref[0]

    def cells_of(t, b):
        t = jnp.where(t >= theta_count, t - theta_count, t)
        return all_ref[t * band_count + b].reshape(ncomp, width)

    lane = lax.broadcasted_iota(jnp.int32, (ncomp, width), 1)

    def shifted(row, shift):
        start = theta * width + shift
        first = lax.rem(start // width, theta_count)
        skip = lax.rem(start, width)
        back = lax.rem(width - skip, width)
        one = pltpu.roll(cells_of(first, row), back, 1)
        two = pltpu.roll(cells_of(first + 1, row), back, 1)
        return jnp.where(lane < width - skip, one, two)

    precond = cells_of(theta, band)
    before = cells_of(theta + theta_count - 1, band)
    after = cells_of(theta + 1, band)
    theta_minus = jnp.where(lane == 0, pltpu.roll(before, 1, 1), pltpu.roll(precond, 1, 1))
    theta_plus = jnp.where(lane == width - 1, pltpu.roll(after, width - 1, 1), pltpu.roll(precond, width - 1, 1))
    up_shift = jnp.where(band == middle - 1, offset, 0)
    low_shift = jnp.where(band == middle, cycle - offset, 0)
    band_plus = shifted(jnp.minimum(band + 1, band_count - 1), up_shift)
    band_plus = jnp.where(band == band_count - 1, 0.0, band_plus)
    band_minus = shifted(jnp.maximum(band - 1, 0), low_shift)
    band_minus = jnp.where(band == 0, 0.0, band_minus)
    image = 6.0 * precond + coupled(jac_ref, precond)
    image = image - (
        face_ref[0, :, 0, :] * theta_minus
        + face_ref[1, :, 0, :] * theta_plus
        + face_ref[2, :, 0, :] * band_minus
        + face_ref[3, :, 0, :] * band_plus
    )
    image_ref[...] = image
    vectors = [basis_ref[i, :, 0, :] for i in range(kb)]
    pairs = [vectors[i] * image for i in range(kb)] + [image * image]
    pairs += [vectors[i] * vectors[j] for i in range(kb) for j in range(kb)]
    rows = jnp.concatenate(over_cells(pairs), axis=0)
    send_ref[...] = jnp.broadcast_to(lane_reduced(rows), send_ref.shape)


def finish_kernel(total, sums_ref, image_ref, basis_ref, next_ref, hess_ref):
    kb = basis_ref.shape[0]
    sums = jnp.sum(sums_ref[...], axis=0, keepdims=True) / total
    proj = [sums[0, i] for i in range(kb)]
    gram = [sums[0, kb + 1 + i] for i in range(kb * kb)]
    finished(proj, gram, sums[0, kb], image_ref[...], basis_ref, next_ref, hess_ref)


def two_exchanges(precond, basis, jac_block, face_coef, rotor_offset):
    kb, ncomp, _, width = basis.shape
    theta_count = lax.axis_size("theta")
    band_count = lax.axis_size("band")
    devices = theta_count * band_count
    copies = jnp.broadcast_to(precond[None], (devices, ncomp, 1, width))
    everyone = lax.all_to_all(copies, AXES, 0, 0, tiled=True)
    image, partial = pl.pallas_call(
        lambda *refs: image_kernel(theta_count, band_count, *refs),
        out_shape=(pltpu.VMEM((ncomp, width), jnp.float32), pltpu.VMEM((devices, width), jnp.float32)),
        in_specs=specs(4, 1),
        out_specs=specs(2),
        name="image",
    )(rotor_offset, *in_vmem(everyone, basis, jac_block, face_coef))
    sums = lax.all_to_all(partial, AXES, 0, 0, tiled=True)
    total = ncomp * devices * width
    return pl.pallas_call(
        lambda *refs: finish_kernel(total, *refs),
        out_shape=(
            jax.ShapeDtypeStruct((ncomp, 1, width), jnp.float32),
            jax.ShapeDtypeStruct((1, kb + 1), jnp.float32),
        ),
        in_specs=specs(3),
        out_specs=specs(2),
        name="finish",
    )(*in_vmem(sums, image, basis))


def thirds(x):
    high = x.astype(jnp.bfloat16).astype(jnp.float32)
    middle = (x - high).astype(jnp.bfloat16).astype(jnp.float32)
    return high, middle, x - high - middle


def shared_pairs(kb, ncomp):
    pairs = [(i, u) for i in range(kb) for u in range(ncomp)]
    count = -(-(kb + 1) * ncomp // 2)
    return pairs[:count], pairs[count:]


def message_rows(kb, ncomp):
    return even(3 * ncomp + 2 + len(shared_pairs(kb, ncomp)[0]))


def places(base, array):
    row = lax.broadcasted_iota(jnp.int32, array.shape, 0)
    lane = lax.broadcasted_iota(jnp.int32, array.shape, 1)
    width = array.shape[1]
    out = jnp.where(lane == base + row, array[:, :1], 0.0)
    return out + jnp.where(lane == base + width // 2 + row, array[:, width - 1 :], 0.0)


def early_kernel(
    basis_hbm, jac_hbm, face_hbm, panel_hbm, offset_hbm, sums_ref, edge_ref, block_ref, basis_ref, face_ref, panel_ref, offset_ref, jac_ref, sems
):
    pairs = ((basis_hbm, basis_ref), (jac_hbm, jac_ref), (face_hbm, face_ref), (panel_hbm, panel_ref), (offset_hbm, offset_ref))
    copies = [pltpu.make_async_copy(source, target, sems.at[i]) for i, (source, target) in enumerate(pairs)]
    for copy in copies:
        copy.start()
    for copy in copies[:3]:
        copy.wait()
    kb, ncomp, _, width = basis_ref.shape
    vectors = [basis_ref[i, :, 0, :] for i in range(kb)]
    pairs = [vectors[i] * vectors[j] for i in range(kb) for j in range(kb)]
    blank = [jnp.zeros((1, width), jnp.float32)] * (kb + 1)
    rows = jnp.concatenate(blank + over_cells(pairs), axis=0)
    high, middle, low = thirds(lane_reduced(rows))
    sums_ref[...] = high + pltpu.roll(middle, THIRD, 1) + pltpu.roll(low, 2 * THIRD, 1)
    row = lax.broadcasted_iota(jnp.int32, (ncomp, width), 0)
    lane = lax.broadcasted_iota(jnp.int32, (ncomp, width), 1)
    edges = jnp.where(lane < width // 2, face_ref[0, :, 0, :], face_ref[1, :, 0, :])
    edge = sum(places(EIGHT * i, array) for i, array in enumerate([edges, *vectors]))
    edge_ref[...] = jnp.sum(edge, axis=0, keepdims=True)
    for w in range(ncomp):
        block_ref[w] = jac_ref[:, w, 0, :] + jnp.where(row == w, 6.0, 0.0)
    copies[3].wait()
    copies[4].wait()


def local_kernel(
    near_ref,
    beyond_ref,
    far_basis_ref,
    far_face_ref,
    panel_ref,
    basis_ref,
    face_ref,
    sums_ref,
    edge_ref,
    block_ref,
    send_ref,
    inner_ref,
    precond_ref,
):
    kb, ncomp, _, width = basis_ref.shape
    half = width // 2
    slot = message_rows(kb, ncomp)
    lane = lax.broadcasted_iota(jnp.int32, (ncomp, width), 1)
    current = basis_ref[kb - 1, :, 0, :]
    swapped = pltpu.roll(current, half, 1)
    near, beyond = near_ref[kb - 1, :, 0, :], beyond_ref[kb - 1, :, 0, :]
    is_low = lax.rem(lax.axis_index("theta"), 2) == 0
    left = jnp.where(lane < half, pltpu.roll(jnp.where(is_low, beyond, near), half, 1), swapped)
    right = jnp.where(lane < half, swapped, pltpu.roll(jnp.where(is_low, near, beyond), half, 1))
    owned = []
    for h, cells in enumerate((left, right)):
        vector = jnp.concatenate([jnp.broadcast_to(cells[u : u + 1], (8, width)) for u in range(ncomp)], axis=1)
        owned.append(
            lax.dot_general(
                vector.astype(jnp.bfloat16),
                panel_ref[0, h],
                (((1,), (1,)), ((), ())),
                preferred_element_type=jnp.float32,
            )[:1]
        )
    halves = [[owned[h][:, u * half : (u + 1) * half] for u in range(ncomp)] for h in range(2)]
    precond = jnp.concatenate([jnp.concatenate([halves[0][u], halves[1][u]], axis=1) for u in range(ncomp)], axis=0)
    precond_ref[...] = precond
    lower = jnp.where(lane == 0, 0.0, pltpu.roll(precond, 1, 1))
    upper = jnp.where(lane == width - 1, 0.0, pltpu.roll(precond, width - 1, 1))
    inner = block_ref[0] * precond[0:1]
    for w in range(1, ncomp):
        inner += block_ref[w] * precond[w : w + 1]
    inner = inner - (face_ref[0, :, 0, :] * lower + face_ref[1, :, 0, :] * upper)
    inner_ref[...] = inner
    band = lax.axis_index("band")
    is_even = lax.rem(band, 2) == 0
    beside = jnp.logical_or(band == 1, band == 2)
    lower_face, upper_face = face_ref[2, :, 0, :], face_ref[3, :, 0, :]
    to_partner = jnp.where(is_even, upper_face, lower_face)
    to_rotor = jnp.where(is_even, lower_face, upper_face)
    reach = jnp.where(is_even, far_face_ref[2, :, 0, :], far_face_ref[3, :, 0, :]) * precond
    pairs = [basis_ref[i, :, 0, :] * inner - far_basis_ref[i, :, 0, :] * reach for i in range(kb)] + [inner * inner]
    high, middle, low = thirds(lane_reduced(jnp.concatenate(over_cells(pairs), axis=0)))
    sums = sums_ref[...] + high + pltpu.roll(middle, THIRD, 1) + pltpu.roll(low, 2 * THIRD, 1)
    carried, kept = shared_pairs(kb, ncomp)
    for_partner = jnp.concatenate([far_basis_ref[i, u : u + 1, 0, :] for i, u in carried], axis=0)
    spare = [jnp.zeros((1, width), jnp.float32)] * (len(carried) - ncomp - len(kept))
    own_part = jnp.concatenate([to_rotor] + [basis_ref[i, u : u + 1, 0, :] for i, u in kept] + spare, axis=0)
    groups = [to_partner, inner, precond, sums, edge_ref[...], jnp.where(beside, own_part, for_partner)]
    filled = 3 * ncomp + 2 + len(carried)
    if slot > filled:
        groups.append(jnp.zeros((slot - filled, width), jnp.float32))
    message = jnp.concatenate(groups, axis=0).astype(jnp.bfloat16)
    for device in range(send_ref.shape[0] // slot):
        send_ref[device * slot : (device + 1) * slot] = message


def merged_kernel(theta_count, band_count, offset_ref, all_ref, inner_ref, precond_ref, basis_ref, face_ref, out_ref, next_ref, hess_ref, own_ref):
    kb, ncomp, _, width = basis_ref.shape
    out_ref[:, 0, :] = precond_ref[...]
    devices = theta_count * band_count
    cycle = theta_count * width
    total = ncomp * devices * width
    middle = band_count // 2
    shape = (devices, width)
    row = lax.broadcasted_iota(jnp.int32, shape, 0)
    lane = lax.broadcasted_iota(jnp.int32, shape, 1)
    band = lax.rem(row, band_count)
    here = lax.axis_index("theta") * band_count + lax.axis_index("band")
    base = cycle // 2 - width
    start = offset_ref[0] - base
    late = start >= width
    skip = jnp.where(late, start - width, start)

    def part(place):
        return all_ref[pl.ds(place, devices, stride=all_ref.shape[0] // devices), :]

    def rows_up(x, count):
        return pltpu.roll(x, (devices - count) % devices, 0)

    half = theta_count // 2
    is_even = lax.rem(band, 2) == 0
    beside = jnp.logical_or(band == middle - 1, band == middle)
    local, edge_row = part(3 * ncomp), part(3 * ncomp + 1)
    tail = 3 * ncomp + 2
    square = jnp.zeros(shape, jnp.float32)
    at_edges = jnp.zeros(shape, jnp.float32)
    turns, handed = [], []
    for u in range(ncomp):
        inner, precond = part(ncomp + u), part(2 * ncomp + u)
        turned = pltpu.roll(precond, lax.rem(width - skip, width), 1)
        near, at, far = (rows_up(turned, (half + k) * band_count + 1) for k in (-1, 0, 1))
        split = lane < width - skip
        rotor_up = jnp.where(split, jnp.where(late, at, near), jnp.where(late, far, at))
        turned = pltpu.roll(precond, skip, 1)
        near, at, far = (rows_up(turned, (-half + k) * band_count - 1) for k in (1, 0, -1))
        split = lane >= skip
        rotor_down = jnp.where(split, jnp.where(late, at, near), jnp.where(late, far, at))
        rotor = jnp.where(band == middle - 1, rotor_up, jnp.where(band == middle, rotor_down, 0.0))
        partner = jnp.where(is_even, rows_up(precond, 1), rows_up(precond, -1))
        before = rows_up(pltpu.roll(precond, 1, 1), -band_count)
        after = rows_up(pltpu.roll(precond, width - 1, 1), band_count)
        edge = jnp.where(lane == 0, before, after)
        first = pltpu.roll(edge_row, (width - u) % width, 1)
        last = pltpu.roll(edge_row, width - 1 - width // 2 - u, 1)
        coef = jnp.where(lane == 0, first, jnp.where(lane == width - 1, last, 0.0))
        own_ref[0, u] = partner
        own_ref[1, u] = rotor
        own_ref[2, u] = edge
        rim = coef * edge
        turn = part(tail + u) * rotor
        turns.append(turn)
        handed.append(jnp.where(is_even, rows_up(turn, 1), rows_up(turn, -1)))
        outer = part(u) * partner + turn + rim
        square += outer * (outer - 2.0 * inner)
        at_edges = jnp.where(lane == u, pltpu.roll(rim, u, 1), at_edges)
        at_edges = jnp.where(lane == width // 2 + u, pltpu.roll(rim, width // 2 + 1 + u, 1), at_edges)
    carried, kept = shared_pairs(kb, ncomp)
    cross = [pltpu.roll(edge_row, width - EIGHT * (i + 1), 1) * at_edges for i in range(kb)]
    in_partner = [jnp.zeros(shape, jnp.float32) for _ in range(kb)]
    in_own = [jnp.zeros(shape, jnp.float32) for _ in range(kb)]
    for place, (i, u) in enumerate(carried):
        values = handed[u]
        mine = place - ncomp
        if 0 <= mine < len(kept):
            values = jnp.where(beside, turns[kept[mine][1]], values)
        product = part(tail + place) * values
        in_partner[i] += product
        if 0 <= mine < len(kept):
            in_own[kept[mine][0]] += product
    cross = [cross[i] + jnp.where(beside, in_own[i], in_partner[i]) for i in range(kb)]
    local = jnp.sum(local, axis=0, keepdims=True) / total
    local = local + pltpu.roll(local, width - THIRD, 1) + pltpu.roll(local, width - 2 * THIRD, 1)
    sums = lane_reduced(jnp.concatenate(over_cells(cross + [square]), axis=0)) / total
    proj = [local[0, i] - sums[0, i] for i in range(kb)]
    gram = [local[0, kb + 1 + i] for i in range(kb * kb)]

    def own(k):
        return own_ref[k, :, pl.ds(here, 1), :].reshape(ncomp, width)

    lane = lax.broadcasted_iota(jnp.int32, (ncomp, width), 1)
    edges = jnp.where(lane == 0, face_ref[0, :, 0, :], jnp.where(lane == width - 1, face_ref[1, :, 0, :], 0.0))
    is_even = lax.rem(lax.axis_index("band"), 2) == 0
    lower_face, upper_face = face_ref[2, :, 0, :], face_ref[3, :, 0, :]
    outer = jnp.where(is_even, upper_face, lower_face) * own(0) + edges * own(2)
    outer += jnp.where(is_even, lower_face, upper_face) * own(1)
    finished(proj, gram, local[0, kb] + sums[0, kb], inner_ref[...] - outer, basis_ref, next_ref, hess_ref)


def one_exchange(near, beyond, far, panel_inverse, basis, jac_block, face_coef, rotor_offset):
    kb, ncomp, _, width = basis.shape
    theta_count = lax.axis_size("theta")
    band_count = lax.axis_size("band")
    devices = theta_count * band_count
    anywhere = pl.BlockSpec(memory_space=pl.ANY)
    *early, basis, face_coef, panel_inverse, rotor_offset = pl.pallas_call(
        early_kernel,
        out_shape=(
            pltpu.VMEM((1, width), jnp.float32),
            pltpu.VMEM((1, width), jnp.float32),
            pltpu.VMEM((ncomp, ncomp, width), jnp.float32),
            pltpu.VMEM(basis.shape, basis.dtype),
            pltpu.VMEM(face_coef.shape, face_coef.dtype),
            pltpu.VMEM(panel_inverse.shape, panel_inverse.dtype),
            pltpu.SMEM(rotor_offset.shape, rotor_offset.dtype),
        ),
        in_specs=[anywhere] * 5,
        out_specs=specs(6) + specs(0, 1),
        scratch_shapes=[pltpu.VMEM(jac_block.shape, jac_block.dtype), pltpu.SemaphoreType.DMA((5,))],
        name="early",
    )(basis, jac_block, face_coef, panel_inverse, rotor_offset)
    send, inner, precond = pl.pallas_call(
        local_kernel,
        out_shape=(
            pltpu.VMEM((devices * message_rows(kb, ncomp), width), jnp.bfloat16),
            pltpu.VMEM((ncomp, width), jnp.float32),
            pltpu.VMEM((ncomp, width), jnp.float32),
        ),
        in_specs=specs(10),
        out_specs=specs(3),
        name="local",
    )(*in_vmem(near, beyond, *far, panel_inverse, basis, face_coef, *early))
    everyone = exchanged(send, devices)
    everyone = everyone.astype(jnp.float32)
    return pl.pallas_call(
        lambda *refs: merged_kernel(theta_count, band_count, *refs),
        out_shape=(
            jax.ShapeDtypeStruct((ncomp, 1, width), jnp.float32),
            jax.ShapeDtypeStruct((ncomp, 1, width), jnp.float32),
            jax.ShapeDtypeStruct((1, kb + 1), jnp.float32),
        ),
        in_specs=specs(5, 1),
        out_specs=specs(3),
        scratch_shapes=[pltpu.VMEM((3, ncomp, devices, width), jnp.float32)],
        name="merged",
    )(rotor_offset, *in_vmem(everyone, inner, precond, basis, face_coef))


def exchanged(rows, devices):
    slots = rows.reshape(devices, -1, 2, rows.shape[-1])
    return lax.all_to_all(slots, AXES, 0, 0, tiled=True).reshape(rows.shape)


def on_device(basis, jac_block, face_coef, panel_inverse, rotor_offset):
    kb, ncomp, rows_here, width = basis.shape
    assert rows_here == 1
    half = width // 2
    theta_count = lax.axis_size("theta")
    band_count = lax.axis_size("band")
    up = [(i, (i + 1) % theta_count) for i in range(theta_count)]
    down = [(j, i) for i, j in up]
    if theta_count * band_count <= MERGED_LIMIT and band_count == 4 and theta_count % 2 == 0:
        pairs = [(b, b + 1 - 2 * (b % 2)) for b in range(band_count)]
        far_basis = lax.ppermute(basis, "band", pairs)
        far = [far_basis, lax.ppermute(face_coef, "band", pairs)]
        near = lax.ppermute(basis, "theta", [(t, t + 1 - 2 * (t % 2)) for t in range(theta_count)])
        turned = [(t, (t - 1 + 2 * (t % 2)) % theta_count) for t in range(theta_count)]
        beyond = lax.ppermute(basis, "theta", turned)
        precond, v_next, hess = one_exchange(near, beyond, far, panel_inverse, basis, jac_block, face_coef, rotor_offset)
        return precond, v_next, hess.reshape(kb + 1)
    before = lax.ppermute(basis, "theta", up)
    after = lax.ppermute(basis, "theta", down)
    before, current, after = (x[-1].astype(jnp.bfloat16) for x in (before, basis, after))
    extended = jnp.concatenate([before[..., half:], current, after[..., :half]], axis=2)
    panels = extended.reshape(ncomp, 2, width).transpose(1, 0, 2).reshape(2, ncomp * width)
    owned = jnp.einsum("pij,pj->pi", panel_inverse[0], panels, preferred_element_type=jnp.float32)
    precond = owned.reshape(2, ncomp, half).transpose(1, 0, 2).reshape(ncomp, 1, width)
    v_next, hess = two_exchanges(precond, basis, jac_block, face_coef, rotor_offset)
    return precond, v_next, hess.reshape(kb + 1)


def solution(mesh):
    return jax.shard_map(
        on_device,
        mesh=mesh,
        in_specs=(
            P(None, None, "band", "theta"),
            P(None, None, "band", "theta"),
            P(None, None, "band", "theta"),
            P("band", "theta", None, None),
            P(),
        ),
        out_specs=(P(None, "band", "theta"), P(None, "band", "theta"), P()),
        check_vma=False,
    )
```

```python
import jax
import jax.numpy as jnp
from jax import lax
from jax.experimental import pallas as pl
from jax.experimental.pallas import tpu as pltpu
from jax.sharding import PartitionSpec as P


AXES = ("theta", "band")
MERGED_LIMIT = 64


def even(count):
    return -(-count // 2) * 2


def in_vmem(*arrays):
    return [pltpu.with_memory_space_constraint(array, pltpu.VMEM) for array in arrays]


def specs(count, scalars=0):
    smem = pl.BlockSpec(memory_space=pltpu.SMEM)
    vmem = pl.BlockSpec(memory_space=pltpu.VMEM)
    return [smem] * scalars + [vmem] * count


def lane_reduced(rows):
    count, width = rows.shape
    sums = jnp.sum(rows, axis=1, keepdims=True)
    row = lax.broadcasted_iota(jnp.int32, (count, width), 0)
    lane = lax.broadcasted_iota(jnp.int32, (count, width), 1)
    return jnp.sum(jnp.where(row == lane, sums, 0.0), axis=0, keepdims=True)


def coupled(jac_ref, precond):
    out = jac_ref[:, 0, 0, :] * precond[0:1]
    for w in range(1, precond.shape[0]):
        out += jac_ref[:, w, 0, :] * precond[w : w + 1]
    return out


def over_cells(arrays):
    return [jnp.sum(array, axis=0, keepdims=True) for array in arrays]


def finished(sums, image, basis_ref, next_ref, hess_ref):
    kb = basis_ref.shape[0]
    lane = lax.broadcasted_iota(jnp.int32, sums.shape, 1)
    proj = [sums[:, i : i + 1] for i in range(kb)]
    left, right = jnp.zeros_like(sums), jnp.zeros_like(sums)
    for i in range(kb):
        first = kb + 1 + i * kb
        left = jnp.where(jnp.logical_and(lane >= first, lane < first + kb), proj[i], left)
        column = jnp.logical_and(lane > kb, lax.rem(lane - kb - 1, kb) == i)
        right = jnp.where(column, proj[i], right)
    terms = jnp.where(lane < kb, -2.0 * sums * sums, jnp.where(lane == kb, sums, left * right * sums))
    squares = jnp.sum(terms, axis=1, keepdims=True)
    drop = proj[0] * basis_ref[0, :, 0, :]
    for i in range(1, kb):
        drop += proj[i] * basis_ref[i, :, 0, :]
    hnorm = jnp.sqrt(jnp.broadcast_to(squares + 1e-06, sums.shape))
    next_ref[:, 0, :] = (image - drop) / hnorm
    hess_ref[...] = jnp.where(lane < kb, sums, hnorm)[:, : kb + 1]


def image_kernel(theta_count, band_count, offset_ref, all_ref, basis_ref, jac_ref, face_ref, image_ref, send_ref):
    kb, ncomp, _, width = basis_ref.shape
    cycle = theta_count * width
    middle = band_count // 2
    theta = lax.axis_index("theta")
    band = lax.axis_index("band")
    offset = offset_ref[0]

    def cells_of(t, b):
        t = jnp.where(t >= theta_count, t - theta_count, t)
        return all_ref[t * band_count + b].reshape(ncomp, width)

    lane = lax.broadcasted_iota(jnp.int32, (ncomp, width), 1)

    def shifted(row, shift):
        start = theta * width + shift
        first = lax.rem(start // width, theta_count)
        skip = lax.rem(start, width)
        back = lax.rem(width - skip, width)
        one = pltpu.roll(cells_of(first, row), back, 1)
        two = pltpu.roll(cells_of(first + 1, row), back, 1)
        return jnp.where(lane < width - skip, one, two)

    precond = cells_of(theta, band)
    before = cells_of(theta + theta_count - 1, band)
    after = cells_of(theta + 1, band)
    theta_minus = jnp.where(lane == 0, pltpu.roll(before, 1, 1), pltpu.roll(precond, 1, 1))
    theta_plus = jnp.where(lane == width - 1, pltpu.roll(after, width - 1, 1), pltpu.roll(precond, width - 1, 1))
    up_shift = jnp.where(band == middle - 1, offset, 0)
    low_shift = jnp.where(band == middle, cycle - offset, 0)
    band_plus = shifted(jnp.minimum(band + 1, band_count - 1), up_shift)
    band_plus = jnp.where(band == band_count - 1, 0.0, band_plus)
    band_minus = shifted(jnp.maximum(band - 1, 0), low_shift)
    band_minus = jnp.where(band == 0, 0.0, band_minus)
    image = 6.0 * precond + coupled(jac_ref, precond)
    image = image - (
        face_ref[0, :, 0, :] * theta_minus
        + face_ref[1, :, 0, :] * theta_plus
        + face_ref[2, :, 0, :] * band_minus
        + face_ref[3, :, 0, :] * band_plus
    )
    image_ref[...] = image
    vectors = [basis_ref[i, :, 0, :] for i in range(kb)]
    pairs = [vectors[i] * image for i in range(kb)] + [image * image]
    pairs += [vectors[i] * vectors[j] for i in range(kb) for j in range(kb)]
    rows = jnp.concatenate(over_cells(pairs), axis=0)
    send_ref[...] = jnp.broadcast_to(lane_reduced(rows), send_ref.shape)


def finish_kernel(total, sums_ref, image_ref, basis_ref, next_ref, hess_ref):
    sums = jnp.sum(sums_ref[...], axis=0, keepdims=True) / total
    finished(sums, image_ref[...], basis_ref, next_ref, hess_ref)


def two_exchanges(precond, basis, jac_block, face_coef, rotor_offset):
    kb, ncomp, _, width = basis.shape
    theta_count = lax.axis_size("theta")
    band_count = lax.axis_size("band")
    devices = theta_count * band_count
    copies = jnp.broadcast_to(precond[None], (devices, ncomp, 1, width))
    everyone = lax.all_to_all(copies, AXES, 0, 0, tiled=True)
    image, partial = pl.pallas_call(
        lambda *refs: image_kernel(theta_count, band_count, *refs),
        out_shape=(pltpu.VMEM((ncomp, width), jnp.float32), pltpu.VMEM((devices, width), jnp.float32)),
        in_specs=specs(4, 1),
        out_specs=specs(2),
        name="image",
    )(rotor_offset, *in_vmem(everyone, basis, jac_block, face_coef))
    sums = lax.all_to_all(partial, AXES, 0, 0, tiled=True)
    total = ncomp * devices * width
    return pl.pallas_call(
        lambda *refs: finish_kernel(total, *refs),
        out_shape=(
            jax.ShapeDtypeStruct((ncomp, 1, width), jnp.float32),
            jax.ShapeDtypeStruct((1, kb + 1), jnp.float32),
        ),
        in_specs=specs(3),
        out_specs=specs(2),
        name="finish",
    )(*in_vmem(sums, image, basis))


def sums_lane(kb, ncomp):
    return (kb + 3) * ncomp


def spread(sums, lane):
    high = sums.astype(jnp.bfloat16).astype(jnp.float32)
    return pltpu.roll(high, lane, 1) + pltpu.roll(sums - high, lane + sums.shape[1] // 2, 1)


def shared_pairs(kb, ncomp):
    pairs = [(i, u) for i in range(kb) for u in range(ncomp)]
    count = -(-(kb + 2) * ncomp // 2)
    return pairs[:count], pairs[count:]


def message_rows(kb, ncomp):
    return even(2 * ncomp + 1 + len(shared_pairs(kb, ncomp)[0]))


def places(base, array):
    row = lax.broadcasted_iota(jnp.int32, array.shape, 0)
    lane = lax.broadcasted_iota(jnp.int32, array.shape, 1)
    width = array.shape[1]
    out = jnp.where(lane == base + row, array[:, :1], 0.0)
    return out + jnp.where(lane == base + width // 2 + row, array[:, width - 1 :], 0.0)


def early_kernel(
    basis_hbm, jac_hbm, face_hbm, panel_hbm, offset_hbm, ready_ref, block_ref, basis_ref, face_ref, panel_ref, offset_ref, jac_ref, sems
):
    pairs = ((basis_hbm, basis_ref), (jac_hbm, jac_ref), (face_hbm, face_ref), (panel_hbm, panel_ref), (offset_hbm, offset_ref))
    copies = [pltpu.make_async_copy(source, target, sems.at[i]) for i, (source, target) in enumerate(pairs)]
    for copy in copies:
        copy.start()
    for copy in copies[:3]:
        copy.wait()
    kb, ncomp, _, width = basis_ref.shape
    vectors = [basis_ref[i, :, 0, :] for i in range(kb)]
    pairs = [vectors[i] * vectors[j] for i in range(kb) for j in range(kb)]
    blank = [jnp.zeros((1, width), jnp.float32)] * (kb + 1)
    rows = jnp.concatenate(blank + over_cells(pairs), axis=0)
    sums = spread(lane_reduced(rows), sums_lane(kb, ncomp))
    row = lax.broadcasted_iota(jnp.int32, (ncomp, width), 0)
    lane = lax.broadcasted_iota(jnp.int32, (ncomp, width), 1)
    edges = jnp.where(lane < width // 2, face_ref[0, :, 0, :], face_ref[1, :, 0, :])
    edge = sum(places(ncomp * i, array) for i, array in enumerate([edges, *vectors]))
    is_even = lax.rem(lax.axis_index("band"), 2) == 0
    edge += places(ncomp * (kb + 2), jnp.where(is_even, face_ref[3, :, 0, :], face_ref[2, :, 0, :]))
    ready_ref[...] = sums + jnp.sum(edge, axis=0, keepdims=True)
    for w in range(ncomp):
        block_ref[w] = jac_ref[:, w, 0, :] + jnp.where(row == w, 6.0, 0.0)
    copies[3].wait()
    copies[4].wait()


def local_kernel(
    near_ref,
    beyond_ref,
    far_basis_ref,
    far_face_ref,
    panel_ref,
    basis_ref,
    face_ref,
    ready_ref,
    block_ref,
    send_ref,
    inner_ref,
    precond_ref,
):
    kb, ncomp, _, width = basis_ref.shape
    half = width // 2
    slot = message_rows(kb, ncomp)
    lane = lax.broadcasted_iota(jnp.int32, (ncomp, width), 1)
    current = basis_ref[kb - 1, :, 0, :]
    swapped = pltpu.roll(current, half, 1)
    near, beyond = near_ref[kb - 1, :, 0, :], beyond_ref[kb - 1, :, 0, :]
    is_low = lax.rem(lax.axis_index("theta"), 2) == 0
    left = jnp.where(lane < half, pltpu.roll(jnp.where(is_low, beyond, near), half, 1), swapped)
    right = jnp.where(lane < half, swapped, pltpu.roll(jnp.where(is_low, near, beyond), half, 1))
    owned = []
    for h, cells in enumerate((left, right)):
        vector = jnp.concatenate([jnp.broadcast_to(cells[u : u + 1], (8, width)) for u in range(ncomp)], axis=1)
        owned.append(
            lax.dot_general(
                vector.astype(jnp.bfloat16),
                panel_ref[0, h],
                (((1,), (1,)), ((), ())),
                preferred_element_type=jnp.float32,
            )[:1]
        )
    halves = [[owned[h][:, u * half : (u + 1) * half] for u in range(ncomp)] for h in range(2)]
    precond = jnp.concatenate([jnp.concatenate([halves[0][u], halves[1][u]], axis=1) for u in range(ncomp)], axis=0)
    precond_ref[...] = precond
    lower = jnp.where(lane == 0, 0.0, pltpu.roll(precond, 1, 1))
    upper = jnp.where(lane == width - 1, 0.0, pltpu.roll(precond, width - 1, 1))
    inner = block_ref[0] * precond[0:1]
    for w in range(1, ncomp):
        inner += block_ref[w] * precond[w : w + 1]
    inner = inner - (face_ref[0, :, 0, :] * lower + face_ref[1, :, 0, :] * upper)
    inner_ref[...] = inner
    band = lax.axis_index("band")
    is_even = lax.rem(band, 2) == 0
    beside = jnp.logical_or(band == 1, band == 2)
    lower_face, upper_face = face_ref[2, :, 0, :], face_ref[3, :, 0, :]
    to_partner = jnp.where(is_even, upper_face, lower_face)
    to_rotor = jnp.where(is_even, lower_face, upper_face)
    reach = jnp.where(is_even, far_face_ref[2, :, 0, :], far_face_ref[3, :, 0, :]) * precond
    pairs = [basis_ref[i, :, 0, :] * inner - far_basis_ref[i, :, 0, :] * reach for i in range(kb)]
    pairs.append(inner * inner + jnp.where(beside, reach * reach, 0.0))
    sums = spread(lane_reduced(jnp.concatenate(over_cells(pairs), axis=0)), sums_lane(kb, ncomp))
    edge = ready_ref[...] + sums + jnp.sum(places(ncomp * (kb + 1), inner), axis=0, keepdims=True)
    carried, kept = shared_pairs(kb, ncomp)
    for_partner = jnp.concatenate([far_basis_ref[i, u : u + 1, 0, :] for i, u in carried], axis=0)
    spare = [jnp.zeros((1, width), jnp.float32)] * (len(carried) - 2 * ncomp - len(kept))
    kept_rows = [basis_ref[i, u : u + 1, 0, :] for i, u in kept]
    own_part = jnp.concatenate([to_partner, to_rotor, *kept_rows, *spare], axis=0)
    head = inner * jnp.where(beside, 1.0, to_partner)
    groups = [head, precond, edge, jnp.where(beside, own_part, for_partner)]
    filled = 2 * ncomp + 1 + len(carried)
    if slot > filled:
        groups.append(jnp.zeros((slot - filled, width), jnp.float32))
    message = jnp.concatenate(groups, axis=0).astype(jnp.bfloat16)
    for device in range(send_ref.shape[0] // slot):
        send_ref[device * slot : (device + 1) * slot] = message


def merged_kernel(
    theta_count, band_count, offset_ref, all_ref, inner_ref, precond_ref, basis_ref, face_ref, out_ref, next_ref, hess_ref, own_ref
):
    kb, ncomp, _, width = basis_ref.shape
    out_ref[:, 0, :] = precond_ref[...]
    total = ncomp * theta_count * band_count * width
    slot = all_ref.shape[0] // (theta_count * band_count)
    middle = band_count // 2
    half = theta_count // 2
    side = width // 2
    tail = 2 * ncomp + 1
    bands = range(band_count)
    shape = (theta_count, width)
    lane = lax.broadcasted_iota(jnp.int32, shape, 1)
    start = offset_ref[0] - (theta_count // 2 - 1) * width
    late = start >= width
    skip = jnp.where(late, start - width, start)
    back = lax.rem(width - skip, width)

    def part(band, place):
        return all_ref[pl.ds(band * slot + place, theta_count, stride=band_count * slot), :]

    def around(x, count):
        return pltpu.roll(x, -count % theta_count, 0)

    edge_rows = [part(b, 2 * ncomp) for b in bands]
    zero = jnp.zeros(shape, jnp.float32)
    square = zero
    below, above, gap = [zero] * band_count, [zero] * band_count, [zero] * band_count
    turns = {middle - 1: [], middle: []}
    for u in range(ncomp):
        precond = [part(b, ncomp + u) for b in bands]
        turned = pltpu.roll(precond[middle], back, 1)
        first = jnp.where(late, around(turned, half), around(turned, half - 1))
        rotor_up = jnp.where(lane < width - skip, first, around(first, 1))
        turned = pltpu.roll(precond[middle - 1], skip, 1)
        first = jnp.where(late, around(turned, -half), around(turned, 1 - half))
        rotor = {middle - 1: rotor_up, middle: jnp.where(lane >= skip, first, around(first, -1))}
        for b in bands:
            partner = precond[b + 1 - 2 * (b % 2)]
            own_ref[0, u, b * theta_count : (b + 1) * theta_count] = partner
            head = part(b, u)
            if b in rotor:
                own_ref[1, u, b * theta_count : (b + 1) * theta_count] = rotor[b]
                turns[b].append(part(b, tail + ncomp + u) * rotor[b])
                outer = part(b, tail + u) * partner + turns[b][u]
                square += outer * (outer - 2.0 * head)
                distance = outer - head
                gap[b] = jnp.where(lane == u, pltpu.roll(distance, u, 1), gap[b])
                gap[b] = jnp.where(lane == side + u, pltpu.roll(distance, side + 1 + u, 1), gap[b])
            else:
                square -= 2.0 * head * partner
            below[b] = jnp.where(lane == u, pltpu.roll(precond[b], u + 1, 1), below[b])
            above[b] = jnp.where(lane == side + u, pltpu.roll(precond[b], side + u, 1), above[b])
    cross = [zero] * kb
    carried, kept = shared_pairs(kb, ncomp)
    for b in bands:
        crossing = jnp.where(lane < side, around(below[b], -1), around(above[b], 1))
        if b not in turns:
            other = b + 1 - 2 * (b % 2)
            ends = pltpu.roll(jnp.where(lane < side, below[other], above[other]), side, 1)
            gap[b] = pltpu.roll(edge_rows[b], width - ncomp * (kb + 2), 1) * ends
            gap[b] -= pltpu.roll(edge_rows[b], width - ncomp * (kb + 1), 1)
        own_ref[2, 0, b * theta_count : (b + 1) * theta_count] = crossing
        rim = jnp.where(lax.rem(lane, side) < ncomp, edge_rows[b] * crossing, 0.0)
        square += rim * (rim + 2.0 * gap[b])
        for i in range(kb):
            cross[i] += pltpu.roll(edge_rows[b], width - ncomp * (i + 1), 1) * rim
    for b, turn in turns.items():
        for place, (i, u) in enumerate(carried):
            cross[i] += part(b + 1 - 2 * (b % 2), tail + place) * turn[u]
        for place, (i, u) in enumerate(kept):
            cross[i] += part(b, tail + 2 * ncomp + place) * turn[u]
    local = jnp.sum(sum(edge_rows), axis=0, keepdims=True) / total
    at = sums_lane(kb, ncomp)
    local = pltpu.roll(local, width - at, 1) + pltpu.roll(local, side - at, 1)
    sums = lane_reduced(jnp.concatenate(over_cells(cross + [square]), axis=0)) / total
    place = lax.broadcasted_iota(jnp.int32, sums.shape, 1)
    sums = local + jnp.where(place < kb, -sums, jnp.where(place == kb, sums, 0.0))

    theta, band = lax.axis_index("theta"), lax.axis_index("band")
    here = band * theta_count + theta
    cells = (ncomp, width)
    lane = lax.broadcasted_iota(jnp.int32, cells, 1)
    row = lax.broadcasted_iota(jnp.int32, cells, 0)
    crossing = own_ref[2, 0, pl.ds(here, 1), :]
    lowest = jnp.sum(jnp.where(lane == row, crossing, 0.0), axis=1, keepdims=True)
    highest = jnp.sum(jnp.where(lane == side + row, crossing, 0.0), axis=1, keepdims=True)
    outer = jnp.where(lane == 0, face_ref[0, :, 0, :] * lowest, 0.0)
    outer += jnp.where(lane == width - 1, face_ref[1, :, 0, :] * highest, 0.0)
    is_even = lax.rem(band, 2) == 0
    beside = jnp.logical_or(band == middle - 1, band == middle)
    lower_face, upper_face = face_ref[2, :, 0, :], face_ref[3, :, 0, :]
    outer += jnp.where(is_even, upper_face, lower_face) * own_ref[0, :, pl.ds(here, 1), :].reshape(cells)
    rotor = jnp.where(is_even, lower_face, upper_face) * own_ref[1, :, pl.ds(here, 1), :].reshape(cells)
    outer += jnp.where(beside, rotor, 0.0)
    finished(sums, inner_ref[...] - outer, basis_ref, next_ref, hess_ref)


def one_exchange(near, beyond, far, panel_inverse, basis, jac_block, face_coef, rotor_offset):
    kb, ncomp, _, width = basis.shape
    theta_count = lax.axis_size("theta")
    band_count = lax.axis_size("band")
    devices = theta_count * band_count
    anywhere = pl.BlockSpec(memory_space=pl.ANY)
    *early, basis, face_coef, panel_inverse, rotor_offset = pl.pallas_call(
        early_kernel,
        out_shape=(
            pltpu.VMEM((1, width), jnp.float32),
            pltpu.VMEM((ncomp, ncomp, width), jnp.float32),
            pltpu.VMEM(basis.shape, basis.dtype),
            pltpu.VMEM(face_coef.shape, face_coef.dtype),
            pltpu.VMEM(panel_inverse.shape, panel_inverse.dtype),
            pltpu.SMEM(rotor_offset.shape, rotor_offset.dtype),
        ),
        in_specs=[anywhere] * 5,
        out_specs=specs(5) + specs(0, 1),
        scratch_shapes=[pltpu.VMEM(jac_block.shape, jac_block.dtype), pltpu.SemaphoreType.DMA((5,))],
        name="early",
    )(basis, jac_block, face_coef, panel_inverse, rotor_offset)
    send, inner, precond = pl.pallas_call(
        local_kernel,
        out_shape=(
            pltpu.VMEM((devices * message_rows(kb, ncomp), width), jnp.bfloat16),
            pltpu.VMEM((ncomp, width), jnp.float32),
            pltpu.VMEM((ncomp, width), jnp.float32),
        ),
        in_specs=specs(9),
        out_specs=specs(3),
        name="local",
    )(*in_vmem(near, beyond, *far, panel_inverse, basis, face_coef, *early))
    everyone = exchanged(send, devices)
    everyone = everyone.astype(jnp.float32)
    return pl.pallas_call(
        lambda *refs: merged_kernel(theta_count, band_count, *refs),
        out_shape=(
            jax.ShapeDtypeStruct((ncomp, 1, width), jnp.float32),
            jax.ShapeDtypeStruct((ncomp, 1, width), jnp.float32),
            jax.ShapeDtypeStruct((1, kb + 1), jnp.float32),
        ),
        in_specs=specs(5, 1),
        out_specs=specs(3),
        scratch_shapes=[pltpu.VMEM((3, ncomp, devices, width), jnp.float32)],
        name="merged",
    )(rotor_offset, *in_vmem(everyone, inner, precond, basis, face_coef))


def exchanged(rows, devices):
    slots = rows.reshape(devices, -1, 2, rows.shape[-1])
    return lax.all_to_all(slots, AXES, 0, 0, tiled=True).reshape(rows.shape)


def on_device(basis, jac_block, face_coef, panel_inverse, rotor_offset):
    kb, ncomp, rows_here, width = basis.shape
    assert rows_here == 1
    half = width // 2
    theta_count = lax.axis_size("theta")
    band_count = lax.axis_size("band")
    up = [(i, (i + 1) % theta_count) for i in range(theta_count)]
    down = [(j, i) for i, j in up]
    if theta_count * band_count <= MERGED_LIMIT and band_count == 4 and theta_count % 2 == 0:
        pairs = [(b, b + 1 - 2 * (b % 2)) for b in range(band_count)]
        far_basis = lax.ppermute(basis, "band", pairs)
        far = [far_basis, lax.ppermute(face_coef, "band", pairs)]
        near = lax.ppermute(basis, "theta", [(t, t + 1 - 2 * (t % 2)) for t in range(theta_count)])
        turned = [(t, (t - 1 + 2 * (t % 2)) % theta_count) for t in range(theta_count)]
        beyond = lax.ppermute(basis, "theta", turned)
        precond, v_next, hess = one_exchange(near, beyond, far, panel_inverse, basis, jac_block, face_coef, rotor_offset)
        return precond, v_next, hess.reshape(kb + 1)
    before = lax.ppermute(basis, "theta", up)
    after = lax.ppermute(basis, "theta", down)
    before, current, after = (x[-1].astype(jnp.bfloat16) for x in (before, basis, after))
    extended = jnp.concatenate([before[..., half:], current, after[..., :half]], axis=2)
    panels = extended.reshape(ncomp, 2, width).transpose(1, 0, 2).reshape(2, ncomp * width)
    owned = jnp.einsum("pij,pj->pi", panel_inverse[0], panels, preferred_element_type=jnp.float32)
    precond = owned.reshape(2, ncomp, half).transpose(1, 0, 2).reshape(ncomp, 1, width)
    v_next, hess = two_exchanges(precond, basis, jac_block, face_coef, rotor_offset)
    return precond, v_next, hess.reshape(kb + 1)


def solution(mesh):
    return jax.shard_map(
        on_device,
        mesh=mesh,
        in_specs=(
            P(None, None, "band", "theta"),
            P(None, None, "band", "theta"),
            P(None, None, "band", "theta"),
            P("band", "theta", None, None),
            P(),
        ),
        out_specs=(P(None, "band", "theta"), P(None, "band", "theta"), P()),
        check_vma=False,
    )
```

```python
import jax
import jax.numpy as jnp
from jax import lax
from jax.experimental import pallas as pl
from jax.experimental.pallas import tpu as pltpu
from jax.sharding import PartitionSpec as P


AXES = ("theta", "band")
MERGED_LIMIT = 64


def even(count):
    return -(-count // 2) * 2


def in_vmem(*arrays):
    return [pltpu.with_memory_space_constraint(array, pltpu.VMEM) for array in arrays]


def specs(count, scalars=0):
    smem = pl.BlockSpec(memory_space=pltpu.SMEM)
    vmem = pl.BlockSpec(memory_space=pltpu.VMEM)
    return [smem] * scalars + [vmem] * count


def lane_reduced(rows):
    count, width = rows.shape
    sums = jnp.sum(rows, axis=1, keepdims=True)
    row = lax.broadcasted_iota(jnp.int32, (count, width), 0)
    lane = lax.broadcasted_iota(jnp.int32, (count, width), 1)
    return jnp.sum(jnp.where(row == lane, sums, 0.0), axis=0, keepdims=True)


def coupled(jac_ref, precond):
    out = jac_ref[:, 0, 0, :] * precond[0:1]
    for w in range(1, precond.shape[0]):
        out += jac_ref[:, w, 0, :] * precond[w : w + 1]
    return out


def over_cells(arrays):
    return [jnp.sum(array, axis=0, keepdims=True) for array in arrays]


def finished(sums, image, basis_ref, next_ref, hess_ref):
    kb = basis_ref.shape[0]
    lane = lax.broadcasted_iota(jnp.int32, sums.shape, 1)
    proj = [sums[:, i : i + 1] for i in range(kb)]
    left, right = jnp.zeros_like(sums), jnp.zeros_like(sums)
    for i in range(kb):
        first = kb + 1 + i * kb
        left = jnp.where(jnp.logical_and(lane >= first, lane < first + kb), proj[i], left)
        column = jnp.logical_and(lane > kb, lax.rem(lane - kb - 1, kb) == i)
        right = jnp.where(column, proj[i], right)
    terms = jnp.where(lane < kb, -2.0 * sums * sums, jnp.where(lane == kb, sums, left * right * sums))
    squares = jnp.sum(terms, axis=1, keepdims=True)
    drop = proj[0] * basis_ref[0, :, 0, :]
    for i in range(1, kb):
        drop += proj[i] * basis_ref[i, :, 0, :]
    hnorm = jnp.sqrt(jnp.broadcast_to(squares + 1e-06, sums.shape))
    next_ref[:, 0, :] = (image - drop) / hnorm
    hess_ref[...] = jnp.where(lane < kb, sums, hnorm)[:, : kb + 1]


def image_kernel(theta_count, band_count, offset_ref, all_ref, basis_ref, jac_ref, face_ref, image_ref, send_ref):
    kb, ncomp, _, width = basis_ref.shape
    cycle = theta_count * width
    middle = band_count // 2
    theta = lax.axis_index("theta")
    band = lax.axis_index("band")
    offset = offset_ref[0]

    def cells_of(t, b):
        t = jnp.where(t >= theta_count, t - theta_count, t)
        return all_ref[t * band_count + b].reshape(ncomp, width)

    lane = lax.broadcasted_iota(jnp.int32, (ncomp, width), 1)

    def shifted(row, shift):
        start = theta * width + shift
        first = lax.rem(start // width, theta_count)
        skip = lax.rem(start, width)
        back = lax.rem(width - skip, width)
        one = pltpu.roll(cells_of(first, row), back, 1)
        two = pltpu.roll(cells_of(first + 1, row), back, 1)
        return jnp.where(lane < width - skip, one, two)

    precond = cells_of(theta, band)
    before = cells_of(theta + theta_count - 1, band)
    after = cells_of(theta + 1, band)
    theta_minus = jnp.where(lane == 0, pltpu.roll(before, 1, 1), pltpu.roll(precond, 1, 1))
    theta_plus = jnp.where(lane == width - 1, pltpu.roll(after, width - 1, 1), pltpu.roll(precond, width - 1, 1))
    up_shift = jnp.where(band == middle - 1, offset, 0)
    low_shift = jnp.where(band == middle, cycle - offset, 0)
    band_plus = shifted(jnp.minimum(band + 1, band_count - 1), up_shift)
    band_plus = jnp.where(band == band_count - 1, 0.0, band_plus)
    band_minus = shifted(jnp.maximum(band - 1, 0), low_shift)
    band_minus = jnp.where(band == 0, 0.0, band_minus)
    image = 6.0 * precond + coupled(jac_ref, precond)
    image = image - (
        face_ref[0, :, 0, :] * theta_minus
        + face_ref[1, :, 0, :] * theta_plus
        + face_ref[2, :, 0, :] * band_minus
        + face_ref[3, :, 0, :] * band_plus
    )
    image_ref[...] = image
    vectors = [basis_ref[i, :, 0, :] for i in range(kb)]
    pairs = [vectors[i] * image for i in range(kb)] + [image * image]
    pairs += [vectors[i] * vectors[j] for i in range(kb) for j in range(kb)]
    rows = jnp.concatenate(over_cells(pairs), axis=0)
    send_ref[...] = jnp.broadcast_to(lane_reduced(rows), send_ref.shape)


def finish_kernel(total, sums_ref, image_ref, basis_ref, next_ref, hess_ref):
    sums = jnp.sum(sums_ref[...], axis=0, keepdims=True) / total
    finished(sums, image_ref[...], basis_ref, next_ref, hess_ref)


def two_exchanges(precond, basis, jac_block, face_coef, rotor_offset):
    kb, ncomp, _, width = basis.shape
    theta_count = lax.axis_size("theta")
    band_count = lax.axis_size("band")
    devices = theta_count * band_count
    copies = jnp.broadcast_to(precond[None], (devices, ncomp, 1, width))
    everyone = lax.all_to_all(copies, AXES, 0, 0, tiled=True)
    image, partial = pl.pallas_call(
        lambda *refs: image_kernel(theta_count, band_count, *refs),
        out_shape=(pltpu.VMEM((ncomp, width), jnp.float32), pltpu.VMEM((devices, width), jnp.float32)),
        in_specs=specs(4, 1),
        out_specs=specs(2),
        name="image",
    )(rotor_offset, *in_vmem(everyone, basis, jac_block, face_coef))
    sums = lax.all_to_all(partial, AXES, 0, 0, tiled=True)
    total = ncomp * devices * width
    return pl.pallas_call(
        lambda *refs: finish_kernel(total, *refs),
        out_shape=(
            jax.ShapeDtypeStruct((ncomp, 1, width), jnp.float32),
            jax.ShapeDtypeStruct((1, kb + 1), jnp.float32),
        ),
        in_specs=specs(3),
        out_specs=specs(2),
        name="finish",
    )(*in_vmem(sums, image, basis))


def sums_lane(kb, ncomp):
    return (kb + 4) * ncomp


def spread(sums, lane):
    high = sums.astype(jnp.bfloat16).astype(jnp.float32)
    return pltpu.roll(high, lane, 1) + pltpu.roll(sums - high, lane + sums.shape[1] // 2, 1)


def shared_pairs(kb, ncomp):
    pairs = [(i, u) for i in range(kb) for u in range(ncomp)]
    count = -(-(kb + 1) * ncomp // 2)
    return pairs[:count], pairs[count:]


def message_rows(kb, ncomp):
    return even(2 * ncomp + 1 + len(shared_pairs(kb, ncomp)[0]))


def places(base, array):
    row = lax.broadcasted_iota(jnp.int32, array.shape, 0)
    lane = lax.broadcasted_iota(jnp.int32, array.shape, 1)
    width = array.shape[1]
    out = jnp.where(lane == base + row, array[:, :1], 0.0)
    return out + jnp.where(lane == base + width // 2 + row, array[:, width - 1 :], 0.0)


def early_kernel(
    basis_hbm, jac_hbm, face_hbm, panel_hbm, offset_hbm, ready_ref, block_ref, basis_ref, face_ref, panel_ref, offset_ref, jac_ref, sems
):
    pairs = ((basis_hbm, basis_ref), (jac_hbm, jac_ref), (face_hbm, face_ref), (panel_hbm, panel_ref), (offset_hbm, offset_ref))
    copies = [pltpu.make_async_copy(source, target, sems.at[i]) for i, (source, target) in enumerate(pairs)]
    for copy in copies:
        copy.start()
    for copy in copies[:3]:
        copy.wait()
    kb, ncomp, _, width = basis_ref.shape
    vectors = [basis_ref[i, :, 0, :] for i in range(kb)]
    pairs = [vectors[i] * vectors[j] for i in range(kb) for j in range(kb)]
    blank = [jnp.zeros((1, width), jnp.float32)] * (kb + 1)
    rows = jnp.concatenate(blank + over_cells(pairs), axis=0)
    sums = spread(lane_reduced(rows), sums_lane(kb, ncomp))
    row = lax.broadcasted_iota(jnp.int32, (ncomp, width), 0)
    lane = lax.broadcasted_iota(jnp.int32, (ncomp, width), 1)
    edges = jnp.where(lane < width // 2, face_ref[0, :, 0, :], face_ref[1, :, 0, :])
    edge = sum(places(ncomp * i, array) for i, array in enumerate([edges, *vectors]))
    is_even = lax.rem(lax.axis_index("band"), 2) == 0
    edge += places(ncomp * (kb + 2), jnp.where(is_even, face_ref[3, :, 0, :], face_ref[2, :, 0, :]))
    ready_ref[...] = sums + jnp.sum(edge, axis=0, keepdims=True)
    for w in range(ncomp):
        block_ref[w] = jac_ref[:, w, 0, :] + jnp.where(row == w, 6.0, 0.0)
    copies[3].wait()
    copies[4].wait()


def local_kernel(
    near_ref,
    beyond_ref,
    far_basis_ref,
    far_face_ref,
    panel_ref,
    basis_ref,
    face_ref,
    ready_ref,
    block_ref,
    send_ref,
    inner_ref,
    precond_ref,
):
    kb, ncomp, _, width = basis_ref.shape
    half = width // 2
    slot = message_rows(kb, ncomp)
    lane = lax.broadcasted_iota(jnp.int32, (ncomp, width), 1)
    current = basis_ref[kb - 1, :, 0, :]
    swapped = pltpu.roll(current, half, 1)
    near, beyond = near_ref[kb - 1, :, 0, :], beyond_ref[kb - 1, :, 0, :]
    is_low = lax.rem(lax.axis_index("theta"), 2) == 0
    left = jnp.where(lane < half, pltpu.roll(jnp.where(is_low, beyond, near), half, 1), swapped)
    right = jnp.where(lane < half, swapped, pltpu.roll(jnp.where(is_low, near, beyond), half, 1))
    owned = []
    for h, cells in enumerate((left, right)):
        vector = jnp.concatenate([jnp.broadcast_to(cells[u : u + 1], (8, width)) for u in range(ncomp)], axis=1)
        owned.append(
            lax.dot_general(
                vector.astype(jnp.bfloat16),
                panel_ref[0, h],
                (((1,), (1,)), ((), ())),
                preferred_element_type=jnp.float32,
            )[:1]
        )
    halves = [[owned[h][:, u * half : (u + 1) * half] for u in range(ncomp)] for h in range(2)]
    precond = jnp.concatenate([jnp.concatenate([halves[0][u], halves[1][u]], axis=1) for u in range(ncomp)], axis=0)
    precond_ref[...] = precond
    lower = jnp.where(lane == 0, 0.0, pltpu.roll(precond, 1, 1))
    upper = jnp.where(lane == width - 1, 0.0, pltpu.roll(precond, width - 1, 1))
    inner = block_ref[0] * precond[0:1]
    for w in range(1, ncomp):
        inner += block_ref[w] * precond[w : w + 1]
    inner = inner - (face_ref[0, :, 0, :] * lower + face_ref[1, :, 0, :] * upper)
    inner_ref[...] = inner
    band = lax.axis_index("band")
    is_even = lax.rem(band, 2) == 0
    beside = jnp.logical_or(band == 1, band == 2)
    lower_face, upper_face = face_ref[2, :, 0, :], face_ref[3, :, 0, :]
    to_partner = jnp.where(is_even, upper_face, lower_face)
    to_rotor = jnp.where(is_even, lower_face, upper_face)
    reach = jnp.where(is_even, far_face_ref[2, :, 0, :], far_face_ref[3, :, 0, :]) * precond
    pairs = [basis_ref[i, :, 0, :] * inner - far_basis_ref[i, :, 0, :] * reach for i in range(kb)]
    pairs.append(inner * inner + jnp.where(beside, reach * reach, 0.0))
    sums = spread(lane_reduced(jnp.concatenate(over_cells(pairs), axis=0)), sums_lane(kb, ncomp))
    dynamic = places(ncomp * (kb + 1), inner) + places(ncomp * (kb + 3), precond)
    edge = ready_ref[...] + sums + jnp.sum(dynamic, axis=0, keepdims=True)
    carried, kept = shared_pairs(kb, ncomp)
    for_partner = jnp.concatenate([far_basis_ref[i, u : u + 1, 0, :] for i, u in carried], axis=0)
    spare = [jnp.zeros((1, width), jnp.float32)] * (len(carried) - ncomp - len(kept))
    kept_rows = [basis_ref[i, u : u + 1, 0, :] for i, u in kept]
    own_part = jnp.concatenate([to_rotor, *kept_rows, *spare], axis=0)
    head = inner * jnp.where(beside, 1.0, to_partner)
    groups = [head, jnp.where(beside, precond, reach), edge, jnp.where(beside, own_part, for_partner)]
    filled = 2 * ncomp + 1 + len(carried)
    if slot > filled:
        groups.append(jnp.zeros((slot - filled, width), jnp.float32))
    message = jnp.concatenate(groups, axis=0).astype(jnp.bfloat16)
    for device in range(send_ref.shape[0] // slot):
        send_ref[device * slot : (device + 1) * slot] = message


def merged_kernel(
    theta_count, band_count, offset_ref, all_ref, inner_ref, precond_ref, basis_ref, face_ref, out_ref, next_ref, hess_ref, own_ref
):
    kb, ncomp, _, width = basis_ref.shape
    out_ref[:, 0, :] = precond_ref[...]
    total = ncomp * theta_count * band_count * width
    slot = all_ref.shape[0] // (theta_count * band_count)
    middle = band_count // 2
    half = theta_count // 2
    side = width // 2
    tail = 2 * ncomp + 1
    bands = range(band_count)
    shape = (theta_count, width)
    lane = lax.broadcasted_iota(jnp.int32, shape, 1)
    start = offset_ref[0] - (theta_count // 2 - 1) * width
    late = start >= width
    skip = jnp.where(late, start - width, start)
    back = lax.rem(width - skip, width)

    def part(band, place):
        return all_ref[pl.ds(band * slot + place, theta_count, stride=band_count * slot), :]

    def around(x, count):
        return pltpu.roll(x, -count % theta_count, 0)

    edge_rows = [part(b, 2 * ncomp) for b in bands]
    zero = jnp.zeros(shape, jnp.float32)
    square = zero
    gap = [zero] * band_count
    turns = {middle - 1: [], middle: []}
    for u in range(ncomp):
        precond = [part(b, ncomp + u) for b in bands]
        turned = pltpu.roll(precond[middle], back, 1)
        first = jnp.where(late, around(turned, half), around(turned, half - 1))
        rotor_up = jnp.where(lane < width - skip, first, around(first, 1))
        turned = pltpu.roll(precond[middle - 1], skip, 1)
        first = jnp.where(late, around(turned, -half), around(turned, 1 - half))
        rotor = {middle - 1: rotor_up, middle: jnp.where(lane >= skip, first, around(first, -1))}
        for b in bands:
            partner = precond[b + 1 - 2 * (b % 2)]
            own_ref[0, u, b * theta_count : (b + 1) * theta_count] = partner
            head = part(b, u)
            if b in rotor:
                own_ref[1, u, b * theta_count : (b + 1) * theta_count] = rotor[b]
                turns[b].append(part(b, tail + u) * rotor[b])
                outer = partner + turns[b][u]
                square += outer * (outer - 2.0 * head)
                distance = outer - head
                gap[b] = jnp.where(lane == u, pltpu.roll(distance, u, 1), gap[b])
                gap[b] = jnp.where(lane == side + u, pltpu.roll(distance, side + 1 + u, 1), gap[b])
            else:
                square -= 2.0 * head * partner
    cross = [zero] * kb
    carried, kept = shared_pairs(kb, ncomp)
    ends_of = [pltpu.roll(edge_rows[b], width - ncomp * (kb + 3), 1) for b in bands]
    for b in bands:
        ends = pltpu.roll(ends_of[b], side, 1)
        crossing = jnp.where(lane < side, around(ends, -1), around(ends, 1))
        if b not in turns:
            gap[b] = pltpu.roll(edge_rows[b], width - ncomp * (kb + 2), 1) * ends_of[b + 1 - 2 * (b % 2)]
            gap[b] -= pltpu.roll(edge_rows[b], width - ncomp * (kb + 1), 1)
        own_ref[2, 0, b * theta_count : (b + 1) * theta_count] = crossing
        rim = jnp.where(lax.rem(lane, side) < ncomp, edge_rows[b] * crossing, 0.0)
        square += rim * (rim + 2.0 * gap[b])
        for i in range(kb):
            cross[i] += pltpu.roll(edge_rows[b], width - ncomp * (i + 1), 1) * rim
    for b, turn in turns.items():
        for place, (i, u) in enumerate(carried):
            cross[i] += part(b + 1 - 2 * (b % 2), tail + place) * turn[u]
        for place, (i, u) in enumerate(kept):
            cross[i] += part(b, tail + ncomp + place) * turn[u]
    local = jnp.sum(sum(edge_rows), axis=0, keepdims=True) / total
    at = sums_lane(kb, ncomp)
    local = pltpu.roll(local, width - at, 1) + pltpu.roll(local, side - at, 1)
    sums = lane_reduced(jnp.concatenate(over_cells(cross + [square]), axis=0)) / total
    place = lax.broadcasted_iota(jnp.int32, sums.shape, 1)
    sums = local + jnp.where(place < kb, -sums, jnp.where(place == kb, sums, 0.0))

    theta, band = lax.axis_index("theta"), lax.axis_index("band")
    here = band * theta_count + theta
    cells = (ncomp, width)
    lane = lax.broadcasted_iota(jnp.int32, cells, 1)
    row = lax.broadcasted_iota(jnp.int32, cells, 0)
    crossing = own_ref[2, 0, pl.ds(here, 1), :]
    lowest = jnp.sum(jnp.where(lane == row, crossing, 0.0), axis=1, keepdims=True)
    highest = jnp.sum(jnp.where(lane == side + row, crossing, 0.0), axis=1, keepdims=True)
    outer = jnp.where(lane == 0, face_ref[0, :, 0, :] * lowest, 0.0)
    outer += jnp.where(lane == width - 1, face_ref[1, :, 0, :] * highest, 0.0)
    is_even = lax.rem(band, 2) == 0
    beside = jnp.logical_or(band == middle - 1, band == middle)
    lower_face, upper_face = face_ref[2, :, 0, :], face_ref[3, :, 0, :]
    across = own_ref[0, :, pl.ds(here, 1), :].reshape(cells)
    outer += jnp.where(beside, across, jnp.where(is_even, upper_face, lower_face) * across)
    rotor = jnp.where(is_even, lower_face, upper_face) * own_ref[1, :, pl.ds(here, 1), :].reshape(cells)
    outer += jnp.where(beside, rotor, 0.0)
    finished(sums, inner_ref[...] - outer, basis_ref, next_ref, hess_ref)


def one_exchange(near, beyond, far, panel_inverse, basis, jac_block, face_coef, rotor_offset):
    kb, ncomp, _, width = basis.shape
    theta_count = lax.axis_size("theta")
    band_count = lax.axis_size("band")
    devices = theta_count * band_count
    anywhere = pl.BlockSpec(memory_space=pl.ANY)
    *early, basis, face_coef, panel_inverse, rotor_offset = pl.pallas_call(
        early_kernel,
        out_shape=(
            pltpu.VMEM((1, width), jnp.float32),
            pltpu.VMEM((ncomp, ncomp, width), jnp.float32),
            pltpu.VMEM(basis.shape, basis.dtype),
            pltpu.VMEM(face_coef.shape, face_coef.dtype),
            pltpu.VMEM(panel_inverse.shape, panel_inverse.dtype),
            pltpu.SMEM(rotor_offset.shape, rotor_offset.dtype),
        ),
        in_specs=[anywhere] * 5,
        out_specs=specs(5) + specs(0, 1),
        scratch_shapes=[pltpu.VMEM(jac_block.shape, jac_block.dtype), pltpu.SemaphoreType.DMA((5,))],
        name="early",
    )(basis, jac_block, face_coef, panel_inverse, rotor_offset)
    send, inner, precond = pl.pallas_call(
        local_kernel,
        out_shape=(
            pltpu.VMEM((devices * message_rows(kb, ncomp), width), jnp.bfloat16),
            pltpu.VMEM((ncomp, width), jnp.float32),
            pltpu.VMEM((ncomp, width), jnp.float32),
        ),
        in_specs=specs(9),
        out_specs=specs(3),
        name="local",
    )(*in_vmem(near, beyond, *far, panel_inverse, basis, face_coef, *early))
    everyone = exchanged(send, devices)
    everyone = everyone.astype(jnp.float32)
    return pl.pallas_call(
        lambda *refs: merged_kernel(theta_count, band_count, *refs),
        out_shape=(
            jax.ShapeDtypeStruct((ncomp, 1, width), jnp.float32),
            jax.ShapeDtypeStruct((ncomp, 1, width), jnp.float32),
            jax.ShapeDtypeStruct((1, kb + 1), jnp.float32),
        ),
        in_specs=specs(5, 1),
        out_specs=specs(3),
        scratch_shapes=[pltpu.VMEM((3, ncomp, devices, width), jnp.float32)],
        name="merged",
    )(rotor_offset, *in_vmem(everyone, inner, precond, basis, face_coef))


def exchanged(rows, devices):
    slots = rows.reshape(devices, -1, 2, rows.shape[-1])
    return lax.all_to_all(slots, AXES, 0, 0, tiled=True).reshape(rows.shape)


def on_device(basis, jac_block, face_coef, panel_inverse, rotor_offset):
    kb, ncomp, rows_here, width = basis.shape
    assert rows_here == 1
    half = width // 2
    theta_count = lax.axis_size("theta")
    band_count = lax.axis_size("band")
    up = [(i, (i + 1) % theta_count) for i in range(theta_count)]
    down = [(j, i) for i, j in up]
    if theta_count * band_count <= MERGED_LIMIT and band_count == 4 and theta_count % 2 == 0:
        pairs = [(b, b + 1 - 2 * (b % 2)) for b in range(band_count)]
        far_basis = lax.ppermute(basis, "band", pairs)
        far = [far_basis, lax.ppermute(face_coef, "band", pairs)]
        near = lax.ppermute(basis, "theta", [(t, t + 1 - 2 * (t % 2)) for t in range(theta_count)])
        turned = [(t, (t - 1 + 2 * (t % 2)) % theta_count) for t in range(theta_count)]
        beyond = lax.ppermute(basis, "theta", turned)
        precond, v_next, hess = one_exchange(near, beyond, far, panel_inverse, basis, jac_block, face_coef, rotor_offset)
        return precond, v_next, hess.reshape(kb + 1)
    before = lax.ppermute(basis, "theta", up)
    after = lax.ppermute(basis, "theta", down)
    before, current, after = (x[-1].astype(jnp.bfloat16) for x in (before, basis, after))
    extended = jnp.concatenate([before[..., half:], current, after[..., :half]], axis=2)
    panels = extended.reshape(ncomp, 2, width).transpose(1, 0, 2).reshape(2, ncomp * width)
    owned = jnp.einsum("pij,pj->pi", panel_inverse[0], panels, preferred_element_type=jnp.float32)
    precond = owned.reshape(2, ncomp, half).transpose(1, 0, 2).reshape(ncomp, 1, width)
    v_next, hess = two_exchanges(precond, basis, jac_block, face_coef, rotor_offset)
    return precond, v_next, hess.reshape(kb + 1)


def solution(mesh):
    return jax.shard_map(
        on_device,
        mesh=mesh,
        in_specs=(
            P(None, None, "band", "theta"),
            P(None, None, "band", "theta"),
            P(None, None, "band", "theta"),
            P("band", "theta", None, None),
            P(),
        ),
        out_specs=(P(None, "band", "theta"), P(None, "band", "theta"), P()),
        check_vma=False,
    )
```
